128 devices in a mesh: pb: 16 (over z_hi, y, core), ka: 8 (over z_lo, x).
Axes of the slice: x: 4, y: 4, z: 4 (z_hi: 2, z_lo: 2; z = z_hi * 2 + z_lo), core: 2. Of those that a mesh axis runs over, the one named last changes fastest.
Arguments:
- query_features: bfloat16 [128, 192, 256], P('pb'), may hold values from -6 to 6
- key_features: bfloat16 [192, 128, 256], P(None, 'ka'), may hold values from -6 to 6
- pyramid_grad: bfloat16 [24576, 8, 4080], P('pb', 'ka'), may hold values from -13.0639453 to 13.0639453, as said below
- query_image: bfloat16 [128, 192, 256], P('pb', 'ka'), may hold values from -0.0625 to 0.0625
- key_image: bfloat16 [192, 128, 256], P('pb', 'ka'), may hold values from -0.0625 to 0.0625
- conv_weight: bfloat16 [3, 3, 256, 256], replicated, may hold values from -0.125 to 0.125
Outputs:
- query_image_grad: bfloat16 [128, 192, 256], P('pb', 'ka')
- key_image_grad: bfloat16 [192, 128, 256], P('pb', 'ka')
- weight_grad: float32 [3, 3, 256, 256], replicated
The draws below stay inside these ranges and needn't reach their ends.
Inputs may be any that keep to these rules, and one draw needn't show every extreme that they name: pyramid_grad[q, k] holds the four levels of key strip k one after another as described in the reference program.
All inputs are finite; a program needn't handle non-finite values.
Results may differ from the reference program's by a relative error of at most 0.0056.
Values may be sent and summed in bfloat16 or wider, within the bound.
A program may use at most 128 MiB of HBM per device.

```python
import math
import jax
import jax.numpy as jnp
from jax import lax

D = 256
CIN = 256
LEVELS = 4
W = 192
H = 128
KPACK = 4080
N_PB = 16
N_KA = 8


def draw_pyramid_grad(key, part):
    key_noise = jax.random.fold_in(key, 11)
    fine_count = N_PB * W
    position = jnp.arange(KPACK)
    tier = jnp.where(position >= fine_count, 1.0, 0.0)
    tier = tier + jnp.where(position >= fine_count + fine_count // 4, 1.0, 0.0)
    tier = tier + jnp.where(position >= fine_count + fine_count // 4 + fine_count // 16, 1.0, 0.0)
    tier_scale = 4.0 ** tier * (8.0 / math.sqrt(H * W))
    normal_part = jnp.clip(jax.random.normal(key_noise, (H * W, N_KA, KPACK), jnp.float32), -4.0, 4.0)
    return (normal_part * tier_scale).astype(jnp.bfloat16)


def shard_levels(key, extent, split, low, high):
    gain = 1.0
    for dim, blocks in split:
        draws = jax.random.uniform(jax.random.fold_in(jax.random.fold_in(key, 6), dim), (blocks,), jnp.float32, low / len(split), high / len(split))
        gain = gain * jnp.repeat(jnp.exp(draws), extent[dim] // blocks).reshape((-1,) + (1,) * (len(extent) - 1 - dim))
    return gain


def centred(rng, shape, scale, reach, split=(), held_as=jnp.bfloat16):
    array = scale * jax.random.normal(rng, shape, jnp.float32)
    if split:
        array = array * shard_levels(rng, shape, split, -0.22, 0.18)
    return jnp.clip(array, -reach, reach).astype(held_as)


def setup_inputs(seed: int = 0) -> dict:
    seeds = jax.random.split(jax.random.key(seed), 7)
    return {
        "query_features": centred(seeds[0], (H, W, D), 1.0, 6.0, ((0, 16),)),
        "key_features": centred(seeds[1], (W, H, D), 1.0, 6.0, ((1, 8),)),
        "pyramid_grad": draw_pyramid_grad(jax.random.fold_in(seeds[6], 71), 0),
        "query_image": centred(seeds[3], (H, W, CIN), ((2 * H * W) ** -0.5), 0.0625, ((0, 16), (1, 8))),
        "key_image": centred(seeds[4], (W, H, CIN), ((2 * H * W) ** -0.5), 0.0625, ((0, 16), (1, 8))),
        "conv_weight": centred(seeds[5], (3, 3, CIN, D), (9 * CIN) ** -0.5, 0.125),
    }


def pool_levels(strip):
    strip_float = strip.astype(jnp.float32)
    result = []
    for level_index in range(LEVELS):
        factor = 2 ** level_index
        cell_cols, key_rows, channels = strip_float.shape
        pooled = strip_float.reshape(cell_cols // factor, factor, key_rows // factor, factor, channels).mean(axis=(1, 3))
        result.append(pooled.astype(jnp.bfloat16))
    return result


def conv_backward(conv_input, padded_input, padded_grad, kernel):
    tile_rows = padded_grad.shape[0] - 2
    tile_cols = padded_grad.shape[1] - 2
    out_channels = padded_grad.shape[2]
    in_channels = kernel.shape[2]
    interior = padded_grad[1:1 + tile_rows, 1:1 + tile_cols].reshape(-1, out_channels)
    input_acc = jnp.zeros((tile_rows * tile_cols, in_channels), jnp.float32)
    kernel_rows = []
    for row_shift in range(3):
        kernel_row = []
        for col_shift in range(3):
            shifted = padded_grad[2 - row_shift:2 - row_shift + tile_rows, 2 - col_shift:2 - col_shift + tile_cols].reshape(-1, out_channels)
            input_acc = input_acc + lax.dot_general(shifted, kernel[row_shift, col_shift], (((1,), (1,)), ((), ())), preferred_element_type=jnp.float32)
            window = padded_input[row_shift:row_shift + tile_rows, col_shift:col_shift + tile_cols].reshape(-1, in_channels)
            weight_term = lax.dot_general(window, interior, (((0,), (0,)), ((), ())), preferred_element_type=jnp.float32)
            kernel_row.append(weight_term)
        kernel_rows.append(jnp.stack(kernel_row))
    return input_acc.reshape(tile_rows, tile_cols, in_channels), jnp.stack(kernel_rows)


def reference(query_features, key_features, pyramid_grad, query_image, key_image, conv_weight):
    norm_scale = D ** -0.5
    height, width_cells, channels = query_features.shape
    queries = query_features.reshape(height * width_cells, channels)
    key_rows = height // N_KA
    query_acc = jnp.zeros((height * width_cells, channels), jnp.float32)
    strip_list = []
    for strip_index in range(N_KA):
        strip = key_features[:, strip_index * key_rows:(strip_index + 1) * key_rows, :]
        pooled = pool_levels(strip)
        strip_grads = pyramid_grad[:, strip_index, :]
        key_acc = jnp.zeros((width_cells, key_rows, channels), jnp.float32)
        offset = 0
        for level_index in range(LEVELS):
            factor = 2 ** level_index
            grid_rows = key_rows // factor
            grid_cols = width_cells // factor
            cell_count = grid_rows * grid_cols
            grad_block = strip_grads[:, offset:offset + cell_count]
            offset = offset + cell_count
            ordered = jnp.transpose(pooled[level_index], (1, 0, 2)).reshape(cell_count, channels)
            query_acc = query_acc + jnp.dot(grad_block, ordered, preferred_element_type=jnp.float32)
            coarse = lax.dot_general(grad_block, queries, (((0,), (0,)), ((), ())), preferred_element_type=jnp.float32)
            coarse = jnp.transpose(coarse.reshape(grid_rows, grid_cols, channels), (1, 0, 2))
            spread = jnp.broadcast_to(coarse[:, None, :, None, :], (grid_cols, factor, grid_rows, factor, channels)).reshape(width_cells, key_rows, channels)
            key_acc = key_acc + spread / (4.0 ** level_index)
        strip_list.append(key_acc)
    query_grad = (query_acc * norm_scale).reshape(height, width_cells, channels).astype(jnp.bfloat16)
    key_grad = (jnp.concatenate(strip_list, axis=1) * norm_scale).astype(jnp.bfloat16)
    pad_spec = ((1, 1), (1, 1), (0, 0))
    grad_first, weight_first = conv_backward(query_image, jnp.pad(query_image, pad_spec), jnp.pad(query_grad, pad_spec), conv_weight)
    image_second = jnp.transpose(key_image, (1, 0, 2))
    grad_rows = jnp.transpose(key_grad, (1, 0, 2))
    grad_second, weight_second = conv_backward(image_second, jnp.pad(image_second, pad_spec), jnp.pad(grad_rows, pad_spec), conv_weight)
    query_image_grad = grad_first.astype(jnp.bfloat16)
    key_image_grad = jnp.transpose(grad_second, (1, 0, 2)).astype(jnp.bfloat16)
    return query_image_grad, key_image_grad, weight_first + weight_second
```

```python
import jax
import jax.numpy as jnp
from jax import lax
from jax.experimental import pallas as pl
from jax.experimental.pallas import tpu as pltpu
from jax.sharding import PartitionSpec as P

BF = jnp.bfloat16
F32 = jnp.float32
MESH = pl.DeviceIdType.MESH
CELLS = 4080
QN = 1536
QP = 384
ST = 384
NT = (((1,), (1,)), ((), ()))


def dot(a, b):
    return jnp.dot(a, b, preferred_element_type=F32)


def dot_nt(a, b):
    return lax.dot_general(a, b, NT, preferred_element_type=F32)


def div(v, d):
    return lax.shift_right_logical(v * (-(-(1 << 20) // d)), 20)


def col(n):
    return lax.broadcasted_iota(jnp.int32, (n, 1), 0)


def row(n):
    return lax.broadcasted_iota(jnp.int32, (1, n), 1)


def select(src, n, value=1.0):
    wide = lax.broadcasted_iota(jnp.int32, (src.shape[0], n), 1)
    return jnp.where(wide == src, value, 0.0).astype(BF)


def pick(key, n, value):
    tall = lax.broadcasted_iota(jnp.int32, (n, key.shape[1]), 0)
    return jnp.where(tall == key, value, 0.0).astype(BF)


def kernel(
    g_hbm, q_hbm, k_hbm, qi_hbm, ki_hbm, cw_hbm,
    qg_out, kg_out, w_out,
    g, qv, kv, cw, pool, pool_t, mid, fine, kt, qt,
    c0s, c0r, s1, r1, s2, r2, s3, r3,
    stage, colp, rowp, padt, win_t, grad, wacc,
    a0s, a0r, w1, a1s, a1r, a2s, a2r, a3, wfull, ogs,
    in_sem, send_sem, recv_sem,
):
    pb, ka = lax.axis_index("pb"), lax.axis_index("ka")
    core = pb % 2
    cy = (pb // 2) % 4
    zh = pb // 8
    cx = ka % 4
    zl = ka // 4
    cz = zh * 2 + zl

    def device(x, y, z, c):
        return {"pb": ((z // 2) * 4 + y) * 2 + c, "ka": (z % 2) * 4 + x}

    def shift(dim, d):
        return device(
            (cx + d) % 4 if dim == 0 else cx,
            (cy + d) % 4 if dim == 1 else cy,
            (cz + d) % 4 if dim == 2 else cz,
            core,
        )

    other_core = device(cx, cy, cz, 1 - core)
    pb_up = {"pb": (pb + 15) % 16, "ka": ka}
    pb_down = {"pb": (pb + 1) % 16, "ka": ka}
    ka_up = {"pb": pb, "ka": (ka + 7) % 8}
    ka_down = {"pb": pb, "ka": (ka + 1) % 8}

    counter = [0]

    def send(src, dst, dev):
        n = counter[0]
        counter[0] += 1
        copy = pltpu.make_async_remote_copy(
            src_ref=src, dst_ref=dst, send_sem=send_sem.at[n], recv_sem=recv_sem.at[n],
            device_id=dev, device_id_type=MESH,
        )
        copy.start()
        pending.append(copy)
        return copy

    pending = []
    loads = []

    def load(src, dst):
        copy = pltpu.make_async_copy(src, dst, in_sem.at[len(loads)])
        copy.start()
        loads.append(copy)
        return copy

    ld_k = load(k_hbm, kv)
    ld_q = load(q_hbm, qv)
    ld_gc = load(g_hbm.at[pl.ds(3072, 1008)], g.at[pl.ds(3072, 1008)])
    ld_img = [load(qi_hbm, stage.at[0, pl.ds(0, 192)]), load(ki_hbm, stage.at[1, pl.ds(0, 192)])]
    ld_g = [load(g_hbm.at[pl.ds(768 * i, 768)], g.at[pl.ds(768 * i, 768)]) for i in range(4)]
    ld_cw = load(cw_hbm, cw)

    barrier = pltpu.get_barrier_semaphore()
    partners = [other_core, pb_up, pb_down, ka_up, ka_down]
    partners += [shift(dim, d) for dim in range(3) for d in (1, 2, 3)]
    for partner in partners:
        pl.semaphore_signal(barrier, inc=1, device_id=partner, device_id_type=MESH)

    for s in range(4):
        stage[s, 288:ST, :] = jnp.zeros((ST - 288, 256), BF)
    g[CELLS:4096, :] = jnp.zeros((4096 - CELLS, QN), BF)
    pool[CELLS:4096, :] = jnp.zeros((4096 - CELLS, 256), BF)

    rows_of = (8, 12, 8, 12)
    cols_of = (24, 16, 24, 16)

    def tile_index(s, i, j):
        return j * 12 + i if s == 3 else i * cols_of[s] + j

    def halo_cols(s):
        n_r, n_c = rows_of[s], cols_of[s]
        v = col(32)
        i = v & 15
        src = jnp.where(v < 16, tile_index(s, i, 0), tile_index(s, i, n_c - 1))
        src = jnp.where(i < n_r, src, -1)
        colp[s] = dot(select(src, 192), stage[s, 0:192, :]).astype(BF)
        return [
            send(colp.at[s, pl.ds(0, 16)], stage.at[s, pl.ds(208, 16)], ka_up),
            send(colp.at[s, pl.ds(16, 16)], stage.at[s, pl.ds(192, 16)], ka_down),
        ]

    def halo_rows(s):
        n_r, n_c = rows_of[s], cols_of[s]
        v = col(64)
        j = (v & 31) - 1
        i = jnp.where(v < 32, 0, n_r - 1)
        src = tile_index(s, i, j)
        src = jnp.where(j < 0, jnp.where(ka == 0, -1, 192 + i), src)
        src = jnp.where(j == n_c, jnp.where(ka == 7, -1, 208 + i), src)
        src = jnp.where(j > n_c, -1, src)
        rowp[s] = dot(select(src, 224), stage[s, 0:224, :]).astype(BF)
        return [
            send(rowp.at[s, pl.ds(0, 32)], stage.at[s, pl.ds(256, 32)], pb_up),
            send(rowp.at[s, pl.ds(32, 32)], stage.at[s, pl.ds(224, 32)], pb_down),
        ]

    def padded(s):
        n_r, n_c = rows_of[s], cols_of[s]
        v = col(QP)
        ip = div(v, n_c + 2)
        jp = v - ip * (n_c + 2)
        i, j = ip - 1, jp - 1
        src = tile_index(s, i, j)
        src = jnp.where(j < 0, jnp.where(ka == 0, -1, 192 + i), src)
        src = jnp.where(j == n_c, jnp.where(ka == 7, -1, 208 + i), src)
        src = jnp.where(i < 0, jnp.where(pb == 0, -1, 224 + jp), src)
        src = jnp.where(i == n_r, jnp.where(pb == 15, -1, 256 + jp), src)
        src = jnp.where(i > n_r, -1, src)
        return dot(select(src, ST), stage[s]).astype(BF)

    def tap_offset(s, rs, cs):
        pitch = cols_of[s] + 2
        return cs * pitch + rs if s % 2 else rs * pitch + cs

    def pool_keys():
        o = col(256)
        perm = select((o & 15) * 16 + lax.shift_right_logical(o, 4), 256)
        for b in range(12):
            block = dot(perm, kv[256 * b:256 * b + 256, :]).astype(BF)
            for r in range(16):
                pool[192 * r + 16 * b:192 * r + 16 * b + 16, :] = block[16 * r:16 * r + 16, :]
        k = row(512)
        key = lax.shift_right_logical(k & 15, 1) * 16 + lax.shift_right_logical(k, 5)
        mean = pick(key, 128, 0.25)
        for b in range(6):
            block = dot(mean, kv[512 * b:512 * b + 512, :]).astype(BF)
            for r in range(8):
                at = 3072 + 96 * r + 16 * b
                pool[at:at + 16, :] = block[16 * r:16 * r + 16, :]
        k = row(1024)
        key = lax.shift_right_logical(k & 15, 2) * 16 + lax.shift_right_logical(k, 6)
        mean = pick(key, 64, 0.0625)
        for b in range(3):
            block = dot(mean, kv[1024 * b:1024 * b + 1024, :]).astype(BF)
            for r in range(4):
                at = 3840 + 48 * r + 16 * b
                pool[at:at + 16, :] = block[16 * r:16 * r + 16, :]
        k = row(3072)
        key = (lax.shift_right_logical(k, 3) & 1) * 24 + lax.shift_right_logical(k, 7)
        pool[4032:4080, :] = dot(pick(key, 48, 0.015625), kv[...]).astype(BF)
        o = col(256)
        eye = select(o, 256)
        for b in range(16):
            pool_t[:, 256 * b:256 * b + 256] = dot_nt(eye, pool[256 * b:256 * b + 256, :]).astype(BF)

    def coarse_levels():
        c = dot(g[3072:4080, :], qv[...])
        l3 = (c[960:1008, :] * (1.0 / 64.0)).astype(BF)
        v = col(192)
        r = div(v, 48)
        src = lax.shift_right_logical(r, 1) * 24 + lax.shift_right_logical(v - r * 48, 1)
        l2 = (c[768:960, :] * (1.0 / 16.0) + dot(select(src, 48), l3)).astype(BF)
        v = col(768)
        r = div(v, 96)
        src = lax.shift_right_logical(r, 1) * 48 + lax.shift_right_logical(v - r * 96, 1)
        mid[...] = (c[0:768, :] * 0.25 + dot(select(src, 192), l2)).astype(BF)

    def key_chunk(i):
        v = col(768)
        r = div(v, 192)
        src = lax.shift_right_logical(r, 1) * 96 + lax.shift_right_logical(v - r * 192, 1)
        fine[...] = dot(g[768 * i:768 * i + 768, :], qv[...]) + dot(
            select(src, 192), mid[192 * i:192 * i + 192, :]
        )
        for t in range(8):
            for p in range(2):
                for r in range(4):
                    at = 192 * r + 24 * t + 12 * p
                    kt[i, p, t, 12 * r:12 * r + 12, :] = fine[at:at + 12, :]
        c0s[i] = kt[i, 1 - core].astype(BF)
        return send(c0s.at[i], c0r.at[i], other_core)

    def query_chunk(i):
        part = dot(pool_t[...], g[:, 384 * i:384 * i + 384])
        part = jnp.transpose(part)
        for hh in range(2):
            for k in range(8):
                at = 192 * hh + 24 * k
                qt[i, k, 24 * hh:24 * hh + 24, :] = part[at:at + 24, :]

    def along(u):
        return (1, cy, zh) if u < 4 else (0, cx, zl)

    def part_of(u, g_, n, c):
        lanes = slice(128 * c, 128 * c + 128)
        tile = g_ * 4 + n
        if u < 4:
            return kt[u, core, tile, :, lanes]
        return qt[u - 4, tile, :, lanes]

    def mates(u):
        dim, n, _ = along(u)
        flip = n + 1 - 2 * (n % 2)
        mirror = 3 - n
        return ((flip, mirror), (mirror, flip))

    def ring(u, n):
        dim = along(u)[0]
        return device(n if dim == 0 else cx, n if dim == 1 else cy, cz, core)

    def last_mate(u):
        if u < 4:
            return device(cx, cy, (1 - zh) * 2 + zl, core)
        return device(cx, cy, zh * 2 + (1 - zl), core)

    flight = {}

    def step1(u):
        out = []
        for c in range(2):
            first, _ = mates(u)[c]
            flip = first + 1 - 2 * (first % 2)
            beyond = (3 - first) if c == 0 else flip
            for j in range(4):
                n = first if j < 2 else beyond
                s1[u, c, j] = part_of(u, j % 2, n, c).astype(BF)
            out.append(send(s1.at[u, c], r1.at[u, c], ring(u, first)))
        flight[u, 1] = out

    def step2(u):
        out = []
        for c in range(2):
            flight[u, 1][c].wait_recv()
            _, second = mates(u)[c]
            for j in range(2):
                s2[u, c, j] = (part_of(u, j, second, c) + r1[u, c, 2 + j].astype(F32)).astype(BF)
            out.append(send(s2.at[u, c], r2.at[u, c], ring(u, second)))
        flight[u, 2] = out

    def step3(u):
        out = []
        _, n, z = along(u)
        for c in range(2):
            flight[u, 2][c].wait_recv()
            far = part_of(u, 1 - z, n, c) + r1[u, c, 1 - z].astype(F32) + r2[u, c, 1 - z].astype(F32)
            s3[u, c] = far.astype(BF)
            out.append(send(s3.at[u, c], r3.at[u, c], last_mate(u)))
        flight[u, 3] = out

    def finish(u):
        _, n, z = along(u)
        s = 3 if u < 4 else 2
        at = 48 * (u % 4)
        for c in range(2):
            flight[u, 3][c].wait_recv()
            total = part_of(u, z, n, c) + r1[u, c, z].astype(F32) + r2[u, c, z].astype(F32)
            total = (total + r3[u, c].astype(F32)) * 0.0625
            stage[s, at:at + 48, 128 * c:128 * c + 128] = total.astype(BF)

    def core_step(u):
        flight[u, 0].wait_recv()
        kt[u, core] = kt[u, core] + c0r[u].astype(F32)
        step1(u)

    def image_windows(s):
        o = col(256)
        padt[s] = dot_nt(select(o, 256), padded(s)).astype(BF)
        v = col(192)
        if s == 0:
            i = div(v, 24)
            f = i * 26 + (v - i * 24)
        else:
            j = div(v, 12)
            f = (v - j * 12) * 18 + j
        for rs in range(3):
            for cs in range(3):
                sel = select(f + tap_offset(s, rs, cs), QP)
                win_t[s, rs * 3 + cs] = dot_nt(padt[s], sel).astype(BF)

    def weight_part(s, first):
        for t in range(9):
            term = dot(win_t[s, t], stage[s + 2, 0:192, :])
            wacc[256 * t:256 * t + 256, :] = term if first else wacc[256 * t:256 * t + 256, :] + term

    def input_grad(s, slot):
        pad = padded(s)
        v = col(192)
        if s == 2:
            i = div(v, 24)
            f = i * 26 + (v - i * 24)
        else:
            f = lax.shift_right_logical(v, 4) * 18 + (v & 15)
        acc = jnp.zeros((192, 256), F32)
        for rs in range(3):
            for cs in range(3):
                sel = select(f + tap_offset(s, 2 - rs, 2 - cs), QP)
                win = dot(sel, pad).astype(BF)
                at = 256 * (rs * 3 + cs)
                acc = acc + dot_nt(win, cw[at:at + 256, :])
        ogs[slot] = acc.astype(BF)

    ld_k.wait()
    pool_keys()
    for c in ld_img:
        c.wait()
    pl.semaphore_wait(barrier, len(partners))
    hc = [halo_cols(0), halo_cols(1)]
    ld_q.wait()
    ld_gc.wait()
    coarse_levels()
    hr = []
    for slot in range(12):
        if slot < 4:
            ld_g[slot].wait()
            flight[slot, 0] = key_chunk(slot)
        elif slot < 8:
            query_chunk(slot - 4)
            step1(slot)
        if slot == 2:
            for s in range(2):
                for c in hc[s]:
                    c.wait_recv()
                hr.append(halo_rows(s))
        if slot == 8:
            for s in range(2):
                for c in hr[s]:
                    c.wait_recv()
                image_windows(s)
        for u in range(4):
            if slot == u + 1:
                core_step(u)
            if slot == u + 3:
                step2(u)
            if slot == u + 5:
                step3(u)
            v = u + 4
            if slot == v + 2:
                step2(v)
            if slot == v + 4:
                step3(v)
        if slot == 10:
            for u in range(4):
                finish(u)
            hk = halo_cols(3)
            weight_part(1, True)
    for u in range(4, 8):
        finish(u)
    hq = halo_cols(2)
    weight_part(0, False)

    for h in range(2):
        for j in range(3):
            for n in range(4):
                at = 768 * j + 192 * n
                w1[h, j, n] = wacc[at:at + 192, 128 * h:128 * h + 128]
    a0s[...] = w1[1 - core].astype(BF)
    c0 = send(a0s, a0r, other_core)
    for c in hk:
        c.wait_recv()
    hk = halo_rows(3)
    ld_cw.wait()
    c0.wait_recv()
    w1[core] = w1[core] + a0r[...].astype(F32)
    coords = (cx, cy, cz)
    a1s[...] = w1[core].astype(BF)
    f1 = []
    for j in range(3):
        n = coords[j]
        f1.append([
            send(a1s.at[j, (n + d) % 4], a1r.at[j, d - 1], shift(j, d)) for d in (1, 2, 3)
        ])
    for c in hq:
        c.wait_recv()
    hq = halo_rows(2)
    for c in hk:
        c.wait_recv()
    input_grad(3, 1)
    kg_copy = load(ogs.at[1], kg_out)
    f2 = []
    x1 = []
    for j in range(3):
        for c in f1[j]:
            c.wait_recv()
        x = w1[core, j, coords[j]]
        for d in range(3):
            x = x + a1r[j, d].astype(F32)
        w1[core, j, coords[j]] = x
        for n in range(4):
            a2s[j, n] = x[48 * n:48 * n + 48, :].astype(BF)
        b = (j + 1) % 3
        f2.append([
            send(a2s.at[j, (coords[b] + d) % 4], a2r.at[j, d - 1], shift(b, d)) for d in (1, 2, 3)
        ])
    for c in hq:
        c.wait_recv()
    input_grad(2, 0)
    qg_copy = load(ogs.at[0], qg_out)
    f3 = []
    for j in range(3):
        for c in f2[j]:
            c.wait_recv()
        b, e = (j + 1) % 3, (j + 2) % 3
        at = pl.multiple_of(coords[b] * 48, 48)
        y = w1[core, j, coords[j], pl.ds(at, 48), :]
        for d in range(3):
            y = y + a2r[j, d].astype(F32)
        a3[j, 0] = y.astype(BF)
        f3.append([send(a3.at[j, 0], a3.at[j, d], shift(e, d)) for d in (1, 2, 3)])
    f4 = []
    for j in range(3):
        for c in f3[j]:
            c.wait_recv()
        b, e = (j + 1) % 3, (j + 2) % 3
        y = jnp.zeros((48, 128), F32)
        for k in range(4):
            y = y + a3[j, (coords[e] + 4 - k) % 4].astype(F32)
        mine = wfull.at[core, j, coords[j], coords[b]]
        mine[...] = y.astype(BF)
        f4.append([send(mine, mine, shift(b, d)) for d in (1, 2, 3)])
    f5 = []
    for j in range(3):
        for c in f4[j]:
            c.wait_recv()
        mine = wfull.at[core, j, coords[j]]
        f5.append([send(mine, mine, shift(j, d)) for d in (1, 2, 3)])
    f6 = []
    for j in range(3):
        for c in f5[j]:
            c.wait_recv()
        mine = wfull.at[core, j]
        f6.append(send(mine, mine, other_core))
    for c in f6:
        c.wait_recv()
    w_copy = load(wfull, w_out)
    for c in pending:
        c.wait_send()
    for c in (kg_copy, qg_copy, w_copy):
        c.wait()


def vmem(*shape, dtype=BF):
    return pltpu.VMEM(shape, dtype)


def body(query_features, key_features, pyramid_grad, query_image, key_image, conv_weight):
    cells = jnp.transpose(pyramid_grad.reshape(QN, CELLS))
    anywhere = pl.BlockSpec(memory_space=pl.ANY)
    qg, kg, w = pl.pallas_call(
        kernel,
        out_shape=(
            jax.ShapeDtypeStruct((192, 256), BF),
            jax.ShapeDtypeStruct((192, 256), BF),
            jax.ShapeDtypeStruct((2, 3, 4, 4, 48, 128), BF),
        ),
        in_specs=[anywhere] * 6,
        out_specs=[anywhere] * 3,
        scratch_shapes=[
            vmem(4096, QN), vmem(QN, 256), vmem(3072, 256), vmem(2304, 256),
            vmem(4096, 256), vmem(256, 4096), vmem(768, 256), vmem(768, 256, dtype=F32),
            vmem(4, 2, 8, 48, 256, dtype=F32), vmem(4, 8, 48, 256, dtype=F32),
            vmem(4, 8, 48, 256), vmem(4, 8, 48, 256),
            vmem(8, 2, 4, 48, 128), vmem(8, 2, 4, 48, 128),
            vmem(8, 2, 2, 48, 128), vmem(8, 2, 2, 48, 128),
            vmem(8, 2, 48, 128), vmem(8, 2, 48, 128),
            vmem(4, ST, 256), vmem(4, 32, 256), vmem(4, 64, 256),
            vmem(2, 256, QP), vmem(2, 9, 256, 192), vmem(8, 128), vmem(2304, 256, dtype=F32),
            vmem(3, 4, 192, 128), vmem(3, 4, 192, 128), vmem(2, 3, 4, 192, 128, dtype=F32),
            vmem(3, 4, 192, 128), vmem(3, 3, 192, 128),
            vmem(3, 4, 48, 128), vmem(3, 3, 48, 128), vmem(3, 4, 48, 128),
            vmem(2, 3, 4, 4, 48, 128), vmem(2, 192, 256),
            pltpu.SemaphoreType.DMA((16,)),
            pltpu.SemaphoreType.DMA((128,)),
            pltpu.SemaphoreType.DMA((128,)),
        ],
        compiler_params=pltpu.CompilerParams(
            collective_id=0, has_side_effects=True, vmem_limit_bytes=63000 * 1024
        ),
    )(
        cells,
        query_features.reshape(QN, 256),
        key_features.reshape(3072, 256),
        query_image.reshape(192, 256),
        key_image.reshape(192, 256),
        conv_weight.reshape(2304, 256),
    )
    w = jnp.transpose(w.reshape(2, 2304, 128), (1, 0, 2)).reshape(3, 3, 256, 256)
    return qg.reshape(8, 24, 256), kg.reshape(12, 16, 256), w.astype(F32)


def solution(mesh):
    placed = (
        P("pb", None, None),
        P(None, "ka", None),
        P("pb", "ka", None),
        P("pb", "ka", None),
        P("pb", "ka", None),
        P(),
    )
    return jax.shard_map(
        body,
        mesh=mesh,
        in_specs=placed,
        out_specs=(P("pb", "ka", None), P("pb", "ka", None), P()),
        check_vma=False,
    )
```

```python
import jax
import jax.numpy as jnp
from jax import lax
from jax.experimental import pallas as pl
from jax.experimental.pallas import tpu as pltpu
from jax.sharding import PartitionSpec as P

BF = jnp.bfloat16
F32 = jnp.float32
MESH = pl.DeviceIdType.MESH
CELLS = 4080
QN = 1536
VMEM_BYTES = 50 * 1024 * 1024
QP = 384
ST = 384
NT = (((1,), (1,)), ((), ()))


def dot(a, b):
    return jnp.dot(a, b, preferred_element_type=F32)


def dot_nt(a, b):
    return lax.dot_general(a, b, NT, preferred_element_type=F32)


def div(v, d):
    return lax.shift_right_logical(v * (-(-(1 << 20) // d)), 20)


def col(n):
    return lax.broadcasted_iota(jnp.int32, (n, 1), 0)


def row(n):
    return lax.broadcasted_iota(jnp.int32, (1, n), 1)


def select(src, n, value=1.0):
    wide = lax.broadcasted_iota(jnp.int32, (src.shape[0], n), 1)
    return jnp.where(wide == src, value, 0.0).astype(BF)


def pick(key, n, value):
    tall = lax.broadcasted_iota(jnp.int32, (n, key.shape[1]), 0)
    return jnp.where(tall == key, value, 0.0).astype(BF)


def kernel(
    g_hbm, q_hbm, k_hbm, qi_hbm, ki_hbm, cw_hbm,
    og_out, w_out,
    g, qv, kv, cw, pool, pool_t, mid, fine, kt, qt,
    c0r, s1, r1, s2, r2, s3, r3, d0s, d0r,
    eye, perm, mean1, mean2, mean3, up3, up2, up1,
    stage, colp, rowp, padt, win_t, wacc,
    a0r, xs, a1s, a1r, a2s, a2r, a3, a4, a0b, ogs,
    in_sem, send_sem, recv_sem,
):
    pb, ka = lax.axis_index("pb"), lax.axis_index("ka")
    core = pb % 2
    cy = (pb // 2) % 4
    zh = pb // 8
    cx = ka % 4
    zl = ka // 4
    cz = zh * 2 + zl

    def device(x, y, z, c):
        return {"pb": ((z // 2) * 4 + y) * 2 + c, "ka": (z % 2) * 4 + x}

    def shift(dim, d):
        return device(
            (cx + d) % 4 if dim == 0 else cx,
            (cy + d) % 4 if dim == 1 else cy,
            (cz + d) % 4 if dim == 2 else cz,
            core,
        )

    other_core = device(cx, cy, cz, 1 - core)
    pb_up = {"pb": (pb + 15) % 16, "ka": ka}
    pb_down = {"pb": (pb + 1) % 16, "ka": ka}
    ka_up = {"pb": pb, "ka": (ka + 7) % 8}
    ka_down = {"pb": pb, "ka": (ka + 1) % 8}

    loads = []
    used = [0]

    def group():
        used[0] += 1
        return used[0] - 1

    def send(src, dst, dev, k, n, whole):
        pltpu.make_async_remote_copy(
            src_ref=src, dst_ref=dst, send_sem=send_sem.at[k], recv_sem=recv_sem.at[n],
            device_id=dev, device_id_type=MESH,
        ).start()
        return whole, n

    def arrived(item):
        whole, n = item
        pltpu.make_async_copy(whole, whole, recv_sem.at[n]).wait()

    def load(src, dst):
        copy = pltpu.make_async_copy(src, dst, in_sem.at[len(loads)])
        copy.start()
        loads.append(copy)
        return copy

    ld_k = load(k_hbm, kv)
    ld_q = load(q_hbm, qv)
    ld_gc = load(g_hbm.at[pl.ds(3072, 1008)], g.at[pl.ds(3072, 1008)])
    ld_img = [load(qi_hbm, stage.at[0, pl.ds(0, 192)]), load(ki_hbm, stage.at[1, pl.ds(0, 192)])]
    ld_g = [load(g_hbm.at[pl.ds(768 * i, 768)], g.at[pl.ds(768 * i, 768)]) for i in range(4)]
    ld_cw = load(cw_hbm, cw)

    barrier = pltpu.get_barrier_semaphore()
    partners = [other_core, pb_up, pb_down, ka_up, ka_down]
    partners += [shift(dim, d) for dim in range(3) for d in (1, 2, 3)]
    for partner in partners:
        pl.semaphore_signal(barrier, inc=1, device_id=partner, device_id_type=MESH)

    for s in range(4):
        stage[s, 288:ST, :] = jnp.zeros((ST - 288, 256), BF)
    g[CELLS:4096, :] = jnp.zeros((4096 - CELLS, QN), BF)
    pool[CELLS:4096, :] = jnp.zeros((4096 - CELLS, 256), BF)

    rows_of = (8, 12, 8, 12)
    cols_of = (24, 16, 24, 16)

    def tile_index(s, i, j):
        return j * 12 + i if s == 3 else i * cols_of[s] + j

    @jax.named_scope("halo_cols")
    def halo_cols(s):
        n_r, n_c = rows_of[s], cols_of[s]
        v = col(32)
        i = v & 15
        src = jnp.where(v < 16, tile_index(s, i, 0), tile_index(s, i, n_c - 1))
        src = jnp.where(i < n_r, src, -1)
        colp[s] = dot(select(src, 192), stage[s, 0:192, :]).astype(BF)
        n = group()
        whole = stage.at[s, pl.ds(192, 32)]
        send(colp.at[s, pl.ds(0, 16)], stage.at[s, pl.ds(208, 16)], ka_up, 0, n, whole)
        return send(colp.at[s, pl.ds(16, 16)], stage.at[s, pl.ds(192, 16)], ka_down, 0, n, whole)

    @jax.named_scope("halo_rows")
    def halo_rows(s):
        n_r, n_c = rows_of[s], cols_of[s]
        v = col(64)
        j = (v & 31) - 1
        i = jnp.where(v < 32, 0, n_r - 1)
        src = tile_index(s, i, j)
        src = jnp.where(j < 0, jnp.where(ka == 0, -1, 192 + i), src)
        src = jnp.where(j == n_c, jnp.where(ka == 7, -1, 208 + i), src)
        src = jnp.where(j > n_c, -1, src)
        rowp[s] = dot(select(src, 224), stage[s, 0:224, :]).astype(BF)
        n = group()
        whole = stage.at[s, pl.ds(224, 64)]
        send(rowp.at[s, pl.ds(0, 32)], stage.at[s, pl.ds(256, 32)], pb_up, 1, n, whole)
        return send(rowp.at[s, pl.ds(32, 32)], stage.at[s, pl.ds(224, 32)], pb_down, 1, n, whole)

    def padded(s):
        n_r, n_c = rows_of[s], cols_of[s]
        v = col(QP)
        ip = div(v, n_c + 2)
        jp = v - ip * (n_c + 2)
        i, j = ip - 1, jp - 1
        src = tile_index(s, i, j)
        src = jnp.where(j < 0, jnp.where(ka == 0, -1, 192 + i), src)
        src = jnp.where(j == n_c, jnp.where(ka == 7, -1, 208 + i), src)
        src = jnp.where(i < 0, jnp.where(pb == 0, -1, 224 + jp), src)
        src = jnp.where(i == n_r, jnp.where(pb == 15, -1, 256 + jp), src)
        src = jnp.where(i > n_r, -1, src)
        return dot(select(src, ST), stage[s]).astype(BF)

    def tap_offset(s, rs, cs):
        pitch = cols_of[s] + 2
        return cs * pitch + rs if s % 2 else rs * pitch + cs

    flight = {}

    @jax.named_scope("tables")
    def tables():
        o = col(256)
        eye[...] = select(o, 256)
        perm[...] = select((o & 15) * 16 + lax.shift_right_logical(o, 4), 256)
        k = row(512)
        mean1[...] = pick(lax.shift_right_logical(k & 15, 1) * 16 + lax.shift_right_logical(k, 5), 128, 0.25)
        k = row(1024)
        mean2[...] = pick(lax.shift_right_logical(k & 15, 2) * 16 + lax.shift_right_logical(k, 6), 64, 0.0625)
        k = row(3072)
        key = (lax.shift_right_logical(k, 3) & 1) * 24 + lax.shift_right_logical(k, 7)
        mean3[...] = pick(key, 48, 0.015625)
        v = col(192)
        r = div(v, 48)
        up3[...] = select(lax.shift_right_logical(r, 1) * 24 + lax.shift_right_logical(v - r * 48, 1), 48)
        v = col(768)
        r = div(v, 96)
        up2[...] = select(lax.shift_right_logical(r, 1) * 48 + lax.shift_right_logical(v - r * 96, 1), 192)
        v = col(384)
        r = div(v, 192)
        up1[...] = select(lax.shift_right_logical(v - r * 192, 1), 96)

    @jax.named_scope("pool_keys")
    def pool_keys():
        for b in range(12):
            block = dot(perm[...], kv[256 * b:256 * b + 256, :]).astype(BF)
            for r in range(16):
                pool[192 * r + 16 * b:192 * r + 16 * b + 16, :] = block[16 * r:16 * r + 16, :]
        for b in range(6):
            block = dot(mean1[...], kv[512 * b:512 * b + 512, :]).astype(BF)
            for r in range(8):
                at = 3072 + 96 * r + 16 * b
                pool[at:at + 16, :] = block[16 * r:16 * r + 16, :]
        for b in range(3):
            block = dot(mean2[...], kv[1024 * b:1024 * b + 1024, :]).astype(BF)
            for r in range(4):
                at = 3840 + 48 * r + 16 * b
                pool[at:at + 16, :] = block[16 * r:16 * r + 16, :]
        pool[4032:4080, :] = dot(mean3[...], kv[...]).astype(BF)
        for b in range(16):
            pool_t[:, 256 * b:256 * b + 256] = dot_nt(eye[...], pool[256 * b:256 * b + 256, :]).astype(BF)

    @jax.named_scope("coarse_levels")
    def coarse_levels():
        l3 = (dot(g[4032:4080, :], qv[...]) * (1.0 / 64.0)).astype(BF)
        l2 = (dot(g[3840:4032, :], qv[...]) * (1.0 / 16.0) + dot(up3[...], l3)).astype(BF)
        mid[...] = (dot(g[3072:3840, :], qv[...]) * 0.25 + dot(up2[...], l2)).astype(BF)

    @jax.named_scope("key_rows")
    def key_rows(h):
        fine[h % 2] = dot(g[384 * h:384 * h + 384, :], qv[...]) + dot(up1[...], mid[96 * h:96 * h + 96, :])

    def key_tiles(h):
        for t in range(8):
            for p in range(2):
                for r in range(2):
                    at, to = 192 * r + 24 * t + 12 * p, 24 * (h % 2) + 12 * r
                    kt[h // 2, p, t, to:to + 12, :] = fine[h % 2, at:at + 12, :]

    def core_send(i):
        flight[i, 0] = send(kt.at[i, 1 - core], c0r.at[i], other_core, 2, group(), c0r.at[i])

    @jax.named_scope("query_chunk")
    def query_chunk(i):
        part = dot(pool_t[...], g[:, 384 * i:384 * i + 384])
        part = jnp.transpose(part)
        for hh in range(2):
            for k in range(8):
                at = 192 * hh + 24 * k
                qt[i, k, 24 * hh:24 * hh + 24, :] = part[at:at + 24, :]

    def along(u):
        return (1, cy, zh) if u < 4 else (0, cx, zl)

    def part_of(u, g_, n, c):
        lanes = slice(128 * c, 128 * c + 128)
        tile = g_ * 4 + n
        if u < 4:
            return kt[u, core, tile, :, lanes]
        return qt[u - 4, tile, :, lanes]

    def mates(u):
        dim, n, _ = along(u)
        flip = n + 1 - 2 * (n % 2)
        mirror = 3 - n
        return ((flip, mirror), (mirror, flip))

    def ring(u, n):
        dim = along(u)[0]
        return device(n if dim == 0 else cx, n if dim == 1 else cy, cz, core)

    def last_mate(u):
        if u < 4:
            return device(cx, cy, (1 - zh) * 2 + zl, core)
        return device(cx, cy, zh * 2 + (1 - zl), core)

    @jax.named_scope("step1")
    def step1(u):
        sem = group()
        for c in range(2):
            first, _ = mates(u)[c]
            flip = first + 1 - 2 * (first % 2)
            beyond = (3 - first) if c == 0 else flip
            for j in range(4):
                n = first if j < 2 else beyond
                s1[u, c, j] = part_of(u, j % 2, n, c).astype(BF)
            flight[u, 1] = send(s1.at[u, c], r1.at[u, c], ring(u, first), 3, sem, r1.at[u])

    @jax.named_scope("step2")
    def step2(u):
        sem = group()
        arrived(flight[u, 1])
        for c in range(2):
            _, second = mates(u)[c]
            for j in range(2):
                s2[u, c, j] = (part_of(u, j, second, c) + r1[u, c, 2 + j].astype(F32)).astype(BF)
            flight[u, 2] = send(s2.at[u, c], r2.at[u, c], ring(u, second), 4, sem, r2.at[u])

    @jax.named_scope("step3")
    def step3(u):
        sem = group()
        _, n, z = along(u)
        arrived(flight[u, 2])
        for c in range(2):
            far = part_of(u, 1 - z, n, c) + r1[u, c, 1 - z].astype(F32) + r2[u, c, 1 - z].astype(F32)
            s3[u, c] = far.astype(BF)
            flight[u, 3] = send(s3.at[u, c], r3.at[u, c], last_mate(u), 5, sem, r3.at[u])

    @jax.named_scope("finish")
    def finish(u):
        _, n, z = along(u)
        s = 3 if u < 4 else 2
        at = 48 * (u % 4)
        arrived(flight[u, 3])
        for c in range(2):
            total = part_of(u, z, n, c) + r1[u, c, z].astype(F32) + r2[u, c, z].astype(F32)
            total = (total + r3[u, c].astype(F32)) * 0.0625
            stage[s, at:at + 48, 128 * c:128 * c + 128] = total.astype(BF)

    @jax.named_scope("direct")
    def direct():
        n = group()
        for k in range(8):
            d0s[k] = qt[3, k].astype(BF)
        for dz in range(2):
            for dx in range(4):
                if dz + dx:
                    z, x = (zl + dz) % 2, (cx + dx) % 4
                    flight[7, 1] = send(
                        d0s.at[z * 4 + x], d0r.at[dz * 4 + dx - 1], device(x, cy, zh * 2 + z, core), 13, n, d0r
                    )

    @jax.named_scope("direct_finish")
    def direct_finish():
        arrived(flight[7, 1])
        total = qt[3, zl * 4 + cx]
        for k in range(7):
            total = total + d0r[k].astype(F32)
        stage[2, 144:192, :] = (total * 0.0625).astype(BF)

    @jax.named_scope("core_step")
    def core_step(u):
        arrived(flight[u, 0])
        kt[u, core] = kt[u, core] + c0r[u]
        step1(u)

    @jax.named_scope("image_windows")
    def image_windows(s):
        padt[s] = dot_nt(eye[...], padded(s)).astype(BF)
        v = col(192)
        if s == 0:
            i = div(v, 24)
            f = i * 26 + (v - i * 24)
        else:
            j = div(v, 12)
            f = (v - j * 12) * 18 + j
        for rs in range(3):
            for cs in range(3):
                sel = select(f + tap_offset(s, rs, cs), QP)
                win_t[s, rs * 3 + cs] = dot_nt(padt[s], sel).astype(BF)

    @jax.named_scope("weight_part")
    def weight_part(s, first):
        for t in range(9):
            term = dot(win_t[s, t], stage[s + 2, 0:192, :])
            j, k = t // 3, t % 3
            for h in range(2):
                half = term[:, 128 * h:128 * h + 128]
                rows = slice(256 * k, 256 * k + 256)
                wacc[h, j, rows] = half if first else wacc[h, j, rows] + half
            if not first and k == 2:
                f0.append(send(wacc.at[1 - core, j], a0r.at[j], other_core, 6, group(), a0r.at[j]))

    @jax.named_scope("input_grad")
    def input_grad(s, slot):
        pad = padded(s)
        v = col(192)
        if s == 2:
            i = div(v, 24)
            f = i * 26 + (v - i * 24)
        else:
            f = lax.shift_right_logical(v, 4) * 18 + (v & 15)
        acc = jnp.zeros((192, 256), F32)
        for rs in range(3):
            for cs in range(3):
                sel = select(f + tap_offset(s, 2 - rs, 2 - cs), QP)
                win = dot(sel, pad).astype(BF)
                at = 256 * (rs * 3 + cs)
                acc = acc + dot_nt(win, cw[at:at + 256, :])
        ogs[slot] = acc.astype(BF)

    f0 = []
    tables()
    ld_k.wait()
    pool_keys()
    ld_q.wait()
    ld_gc.wait()
    coarse_levels()
    ld_g[0].wait()
    key_rows(0)
    key_rows(1)
    key_tiles(0)
    ld_g[1].wait()
    key_rows(2)
    key_tiles(1)
    for c in ld_img:
        c.wait()
    pl.semaphore_wait(barrier, len(partners))
    core_send(0)
    hc = [halo_cols(0), halo_cols(1)]
    key_rows(3)
    key_tiles(2)
    ld_g[2].wait()
    key_rows(4)
    key_tiles(3)
    core_send(1)
    core_step(0)
    key_rows(5)
    key_tiles(4)
    ld_g[3].wait()
    key_rows(6)
    key_tiles(5)
    core_send(2)
    core_step(1)

    def queries(i):
        query_chunk(i)
        step1(4 + i)

    queries(0)
    core_step(2)
    step2(0)
    key_rows(7)
    key_tiles(6)
    key_tiles(7)
    core_send(3)
    hr = []
    for s in range(2):
        arrived(hc[s])
        hr.append(halo_rows(s))
    queries(1)
    step2(1)
    core_step(3)
    step3(0)
    queries(2)
    step2(2)
    step2(4)
    query_chunk(3)
    direct()
    step2(5)
    step2(3)
    step3(1)
    step3(2)
    step3(4)
    arrived(hr[1])
    image_windows(1)
    step2(6)
    step3(3)
    step3(5)
    arrived(hr[0])
    image_windows(0)
    step3(6)
    for u in range(4):
        finish(u)
    hk = halo_cols(3)
    weight_part(1, True)
    for u in range(4, 7):
        finish(u)
    direct_finish()
    hq = halo_cols(2)
    weight_part(0, False)

    coords = (cx, cy, cz)
    f1 = []
    for j in range(3):
        arrived(f0[j])
        n = coords[j]
        wacc[core, j] = wacc[core, j] + a0r[j]
        for k in range(4):
            a1s[j, k] = wacc[core, j, 192 * k:192 * k + 192].astype(BF)
        sem = group()
        for d in (1, 2, 3):
            last = send(a1s.at[j, (n + d) % 4], a1r.at[j, d - 1], shift(j, d), 7, sem, a1r.at[j])
        f1.append(last)
    arrived(hk)
    hk = halo_rows(3)
    ld_cw.wait()
    f2 = []
    for j in range(3):
        arrived(f1[j])
        x = wacc[core, j, pl.ds(pl.multiple_of(192 * coords[j], 192), 192), :]
        for d in range(3):
            x = x + a1r[j, d].astype(F32)
        xs[j] = x
        for n in range(4):
            a2s[j, n] = x[48 * n:48 * n + 48, :].astype(BF)
        b = (j + 1) % 3
        sem = group()
        for d in (1, 2, 3):
            last = send(a2s.at[j, (coords[b] + d) % 4], a2r.at[j, d - 1], shift(b, d), 8, sem, a2r.at[j])
        f2.append(last)
    arrived(hq)
    hq = halo_rows(2)
    arrived(hk)
    input_grad(3, 1)
    f3 = []
    for j in range(3):
        arrived(f2[j])
        b, e = (j + 1) % 3, (j + 2) % 3
        y = xs[j, pl.ds(pl.multiple_of(coords[b] * 48, 48), 48), :]
        for d in range(3):
            y = y + a2r[j, d].astype(F32)
        a3[j, 0] = y.astype(BF)
        sem = group()
        for d in (1, 2, 3):
            last = send(a3.at[j, 0], a3.at[j, d], shift(e, d), 9, sem, a3.at[j, pl.ds(1, 3)])
        f3.append(last)
    arrived(hq)
    input_grad(2, 0)
    copies = [load(ogs, og_out)]
    f4 = []
    own = []
    for j in range(3):
        arrived(f3[j])
        b, e = (j + 1) % 3, (j + 2) % 3
        y = jnp.zeros((48, 128), F32)
        for k in range(4):
            y = y + a3[j, (coords[e] + 4 - k) % 4].astype(F32)
        a4[j] = y.astype(BF)
        mine = w_out.at[core, j, coords[j], coords[b]]
        sem = group()
        for d in (1, 2, 3):
            last = send(a4.at[j], mine, shift(b, d), 10, sem, a2r.at[j])
        own.append(load(a4.at[j], mine))
        f4.append(last)
    f5 = []
    for j in range(3):
        arrived(f4[j])
        own[j].wait()
        mine = w_out.at[core, j, coords[j]]
        sem = group()
        for d in (1, 2, 3):
            last = send(mine, mine, shift(j, d), 11, sem, a1r.at[j])
        f5.append(last)
    f6 = []
    for j in range(3):
        arrived(f5[j])
        mine = w_out.at[core, j]
        f6.append(send(mine, mine, other_core, 12, group(), mine))
    for j in range(3):
        arrived(f6[j])
    sent = (colp, rowp, c0r, s1, s2, s3, a0r, a1r, a2r, a2r, a2r, a1r, a0b, d0r)
    for k, ref in enumerate(sent):
        pltpu.make_async_copy(ref, ref, send_sem.at[k]).wait()
    copies[0].wait()


def widen(og, w, qg_out, kg_out, w_out, wide, sem):
    copies = [
        pltpu.make_async_copy(og.at[0], qg_out, sem.at[0]),
        pltpu.make_async_copy(og.at[1], kg_out, sem.at[1]),
    ]
    for k in range(6):
        rows = pl.ds(384 * k, 384)
        for h in range(2):
            wide[384 * k:384 * k + 384, 128 * h:128 * h + 128] = w[h, 384 * k:384 * k + 384, :].astype(F32)
        copies.append(pltpu.make_async_copy(wide.at[rows], w_out.at[rows], sem.at[2 + k]))
        if k == 0:
            copies[0].start()
            copies[1].start()
        copies[-1].start()
    for c in copies:
        c.wait()


def vmem(*shape, dtype=BF):
    return pltpu.VMEM(shape, dtype)


def body(query_features, key_features, pyramid_grad, query_image, key_image, conv_weight):
    cells = jnp.transpose(pyramid_grad.reshape(QN, CELLS))
    anywhere = pl.BlockSpec(memory_space=pl.ANY)
    og, w = pl.pallas_call(
        kernel,
        out_shape=(
            jax.ShapeDtypeStruct((2, 192, 256), BF),
            jax.ShapeDtypeStruct((2, 3, 4, 4, 48, 128), BF),
        ),
        in_specs=[pl.BlockSpec(memory_space=pltpu.HBM)] * 6,
        out_specs=[pl.BlockSpec(memory_space=pl.ANY)] * 2,
        scratch_shapes=[
            vmem(4096, QN), vmem(QN, 256), vmem(3072, 256), vmem(2304, 256),
            vmem(4096, 256), vmem(256, 4096), vmem(768, 256), vmem(2, 384, 256, dtype=F32),
            vmem(4, 2, 8, 48, 256, dtype=F32), vmem(4, 8, 48, 256, dtype=F32),
            vmem(4, 8, 48, 256, dtype=F32),
            vmem(7, 2, 4, 48, 128), vmem(7, 2, 4, 48, 128),
            vmem(7, 2, 2, 48, 128), vmem(7, 2, 2, 48, 128),
            vmem(7, 2, 48, 128), vmem(7, 2, 48, 128),
            vmem(8, 48, 256), vmem(7, 48, 256),
            vmem(256, 256), vmem(256, 256), vmem(128, 512), vmem(64, 1024), vmem(48, 3072),
            vmem(192, 48), vmem(768, 192), vmem(384, 96),
            vmem(4, ST, 256), vmem(4, 32, 256), vmem(4, 64, 256),
            vmem(2, 256, QP), vmem(2, 9, 256, 192), vmem(2, 3, 768, 128, dtype=F32),
            vmem(3, 768, 128, dtype=F32), vmem(3, 192, 128, dtype=F32),
            vmem(3, 4, 192, 128), vmem(3, 3, 192, 128),
            vmem(3, 4, 48, 128), vmem(3, 3, 48, 128), vmem(3, 4, 48, 128),
            vmem(3, 48, 128), vmem(3, 4, 4, 48, 128), vmem(2, 192, 256),
            pltpu.SemaphoreType.DMA((14,)),
            pltpu.SemaphoreType.DMA((14,)),
            pltpu.SemaphoreType.DMA((55,)),
        ],
        compiler_params=pltpu.CompilerParams(
            collective_id=0, has_side_effects=True, vmem_limit_bytes=VMEM_BYTES
        ),
    )(
        *[
            pltpu.with_memory_space_constraint(x, pltpu.HBM)
            for x in (
                cells,
                query_features.reshape(QN, 256),
                key_features.reshape(3072, 256),
                query_image.reshape(192, 256),
                key_image.reshape(192, 256),
                conv_weight.reshape(2304, 256),
            )
        ]
    )
    qg, kg, w = pl.pallas_call(
        widen,
        out_shape=(
            jax.ShapeDtypeStruct((192, 256), BF),
            jax.ShapeDtypeStruct((192, 256), BF),
            jax.ShapeDtypeStruct((2304, 256), F32),
        ),
        in_specs=[pl.BlockSpec(memory_space=pltpu.VMEM)] * 2,
        out_specs=[pl.BlockSpec(memory_space=pltpu.HBM)] * 3,
        scratch_shapes=[vmem(2304, 256, dtype=F32), pltpu.SemaphoreType.DMA((8,))],
        compiler_params=pltpu.CompilerParams(vmem_limit_bytes=16 * 1024 * 1024),
    )(og, w.reshape(2, 2304, 128))
    return qg.reshape(8, 24, 256), kg.reshape(12, 16, 256), w.reshape(3, 3, 256, 256)


def solution(mesh):
    placed = (
        P("pb", None, None),
        P(None, "ka", None),
        P("pb", "ka", None),
        P("pb", "ka", None),
        P("pb", "ka", None),
        P(),
    )
    return jax.shard_map(
        body,
        mesh=mesh,
        in_specs=placed,
        out_specs=(P("pb", "ka", None), P("pb", "ka", None), P()),
        check_vma=False,
    )
```

```python
import jax
import jax.numpy as jnp
from jax import lax
from jax.experimental import pallas as pl
from jax.experimental.pallas import tpu as pltpu
from jax.sharding import PartitionSpec as P

BF = jnp.bfloat16
F32 = jnp.float32
MESH = pl.DeviceIdType.MESH
CELLS = 4080
QN = 1536
VMEM_BYTES = 50 * 1024 * 1024
QP = 384
ST = 384
NT = (((1,), (1,)), ((), ()))


def dot(a, b):
    return jnp.dot(a, b, preferred_element_type=F32)


def dot_nt(a, b):
    return lax.dot_general(a, b, NT, preferred_element_type=F32)


def div(v, d):
    return lax.shift_right_logical(v * (-(-(1 << 20) // d)), 20)


def col(n):
    return lax.broadcasted_iota(jnp.int32, (n, 1), 0)


def row(n):
    return lax.broadcasted_iota(jnp.int32, (1, n), 1)


def select(src, n, value=1.0):
    wide = lax.broadcasted_iota(jnp.int32, (src.shape[0], n), 1)
    return jnp.where(wide == src, value, 0.0).astype(BF)


def pick(key, n, value):
    tall = lax.broadcasted_iota(jnp.int32, (n, key.shape[1]), 0)
    return jnp.where(tall == key, value, 0.0).astype(BF)


def kernel(
    g_hbm, q_hbm, k_hbm, qi_hbm, ki_hbm, cw_hbm,
    og_out, w_out,
    g, qv, kv, cw, pool, pool_t, mid, fine, kt, qt,
    c0r, s1, r1, s2, r2, s3, r3, d0s, d0r,
    eye, perm, mean1, mean2, mean3, up3, up2, up1,
    stage, colp, rowp, padt, win_t, wacc,
    a0r, a1s, a1r, a2, a3, a4, ogs,
    in_sem, send_sem, recv_sem,
):
    pb, ka = lax.axis_index("pb"), lax.axis_index("ka")
    core = pb % 2
    cy = (pb // 2) % 4
    zh = pb // 8
    cx = ka % 4
    zl = ka // 4
    cz = zh * 2 + zl

    def device(x, y, z, c):
        return {"pb": ((z // 2) * 4 + y) * 2 + c, "ka": (z % 2) * 4 + x}

    def shift(dim, d):
        return device(
            (cx + d) % 4 if dim == 0 else cx,
            (cy + d) % 4 if dim == 1 else cy,
            (cz + d) % 4 if dim == 2 else cz,
            core,
        )

    other_core = device(cx, cy, cz, 1 - core)
    pb_up = {"pb": (pb + 15) % 16, "ka": ka}
    pb_down = {"pb": (pb + 1) % 16, "ka": ka}
    ka_up = {"pb": pb, "ka": (ka + 7) % 8}
    ka_down = {"pb": pb, "ka": (ka + 1) % 8}

    loads = []
    used = [0]

    def group():
        used[0] += 1
        return used[0] - 1

    def send(src, dst, dev, k, n, whole):
        pltpu.make_async_remote_copy(
            src_ref=src, dst_ref=dst, send_sem=send_sem.at[k], recv_sem=recv_sem.at[n],
            device_id=dev, device_id_type=MESH,
        ).start()
        return whole, n

    def arrived(item):
        whole, n = item
        pltpu.make_async_copy(whole, whole, recv_sem.at[n]).wait()

    def load(src, dst):
        copy = pltpu.make_async_copy(src, dst, in_sem.at[len(loads)])
        copy.start()
        loads.append(copy)
        return copy

    ld_k = load(k_hbm, kv)
    ld_q = load(q_hbm, qv)
    ld_gc = load(g_hbm.at[pl.ds(3072, 1008)], g.at[pl.ds(3072, 1008)])
    ld_img = [load(qi_hbm, stage.at[0, pl.ds(0, 192)]), load(ki_hbm, stage.at[1, pl.ds(0, 192)])]
    ld_g = [load(g_hbm.at[pl.ds(768 * i, 768)], g.at[pl.ds(768 * i, 768)]) for i in range(4)]
    ld_cw = load(cw_hbm, cw)

    barrier = pltpu.get_barrier_semaphore()
    partners = [other_core, pb_up, pb_down, ka_up, ka_down]
    partners += [shift(dim, d) for dim in range(3) for d in (1, 2, 3)]
    for partner in partners:
        pl.semaphore_signal(barrier, inc=1, device_id=partner, device_id_type=MESH)

    for s in range(4):
        stage[s, 288:ST, :] = jnp.zeros((ST - 288, 256), BF)
    g[CELLS:4096, :] = jnp.zeros((4096 - CELLS, QN), BF)
    pool[CELLS:4096, :] = jnp.zeros((4096 - CELLS, 256), BF)

    rows_of = (8, 12, 8, 12)
    cols_of = (24, 16, 24, 16)

    def tile_index(s, i, j):
        return j * 12 + i if s == 3 else i * cols_of[s] + j

    @jax.named_scope("halo_cols")
    def halo_cols(s):
        n_r, n_c = rows_of[s], cols_of[s]
        v = col(32)
        i = v & 15
        src = jnp.where(v < 16, tile_index(s, i, 0), tile_index(s, i, n_c - 1))
        src = jnp.where(i < n_r, src, -1)
        colp[s] = dot(select(src, 192), stage[s, 0:192, :]).astype(BF)
        n = group()
        whole = stage.at[s, pl.ds(192, 32)]
        send(colp.at[s, pl.ds(0, 16)], stage.at[s, pl.ds(208, 16)], ka_up, 0, n, whole)
        return send(colp.at[s, pl.ds(16, 16)], stage.at[s, pl.ds(192, 16)], ka_down, 0, n, whole)

    @jax.named_scope("halo_rows")
    def halo_rows(s):
        n_r, n_c = rows_of[s], cols_of[s]
        v = col(64)
        j = (v & 31) - 1
        i = jnp.where(v < 32, 0, n_r - 1)
        src = tile_index(s, i, j)
        src = jnp.where(j < 0, jnp.where(ka == 0, -1, 192 + i), src)
        src = jnp.where(j == n_c, jnp.where(ka == 7, -1, 208 + i), src)
        src = jnp.where(j > n_c, -1, src)
        rowp[s] = dot(select(src, 224), stage[s, 0:224, :]).astype(BF)
        n = group()
        whole = stage.at[s, pl.ds(224, 64)]
        send(rowp.at[s, pl.ds(0, 32)], stage.at[s, pl.ds(256, 32)], pb_up, 1, n, whole)
        return send(rowp.at[s, pl.ds(32, 32)], stage.at[s, pl.ds(224, 32)], pb_down, 1, n, whole)

    def padded(s):
        n_r, n_c = rows_of[s], cols_of[s]
        v = col(QP)
        ip = div(v, n_c + 2)
        jp = v - ip * (n_c + 2)
        i, j = ip - 1, jp - 1
        src = tile_index(s, i, j)
        src = jnp.where(j < 0, jnp.where(ka == 0, -1, 192 + i), src)
        src = jnp.where(j == n_c, jnp.where(ka == 7, -1, 208 + i), src)
        src = jnp.where(i < 0, jnp.where(pb == 0, -1, 224 + jp), src)
        src = jnp.where(i == n_r, jnp.where(pb == 15, -1, 256 + jp), src)
        src = jnp.where(i > n_r, -1, src)
        return dot(select(src, ST), stage[s]).astype(BF)

    def tap_offset(s, rs, cs):
        pitch = cols_of[s] + 2
        return cs * pitch + rs if s % 2 else rs * pitch + cs

    flight = {}

    @jax.named_scope("tables")
    def tables():
        o = col(256)
        eye[...] = select(o, 256)
        perm[...] = select((o & 15) * 16 + lax.shift_right_logical(o, 4), 256)
        k = row(512)
        mean1[...] = pick(lax.shift_right_logical(k & 15, 1) * 16 + lax.shift_right_logical(k, 5), 128, 0.25)
        k = row(1024)
        mean2[...] = pick(lax.shift_right_logical(k & 15, 2) * 16 + lax.shift_right_logical(k, 6), 64, 0.0625)
        k = row(3072)
        key = (lax.shift_right_logical(k, 3) & 1) * 24 + lax.shift_right_logical(k, 7)
        mean3[...] = pick(key, 48, 0.015625)
        v = col(192)
        r = div(v, 48)
        up3[...] = select(lax.shift_right_logical(r, 1) * 24 + lax.shift_right_logical(v - r * 48, 1), 48)
        v = col(768)
        r = div(v, 96)
        up2[...] = select(lax.shift_right_logical(r, 1) * 48 + lax.shift_right_logical(v - r * 96, 1), 192)
        v = col(384)
        r = div(v, 192)
        up1[...] = select(lax.shift_right_logical(v - r * 192, 1), 96)

    @jax.named_scope("pool_keys")
    def pool_keys():
        for b in range(12):
            block = dot(perm[...], kv[256 * b:256 * b + 256, :]).astype(BF)
            for r in range(16):
                pool[192 * r + 16 * b:192 * r + 16 * b + 16, :] = block[16 * r:16 * r + 16, :]
        for b in range(6):
            block = dot(mean1[...], kv[512 * b:512 * b + 512, :]).astype(BF)
            for r in range(8):
                at = 3072 + 96 * r + 16 * b
                pool[at:at + 16, :] = block[16 * r:16 * r + 16, :]
        for b in range(3):
            block = dot(mean2[...], kv[1024 * b:1024 * b + 1024, :]).astype(BF)
            for r in range(4):
                at = 3840 + 48 * r + 16 * b
                pool[at:at + 16, :] = block[16 * r:16 * r + 16, :]
        pool[4032:4080, :] = dot(mean3[...], kv[...]).astype(BF)
        for b in range(16):
            pool_t[:, 256 * b:256 * b + 256] = dot_nt(eye[...], pool[256 * b:256 * b + 256, :]).astype(BF)

    @jax.named_scope("coarse_levels")
    def coarse_levels():
        l3 = (dot(g[4032:4080, :], qv[...]) * (1.0 / 64.0)).astype(BF)
        l2 = (dot(g[3840:4032, :], qv[...]) * (1.0 / 16.0) + dot(up3[...], l3)).astype(BF)
        mid[...] = (dot(g[3072:3840, :], qv[...]) * 0.25 + dot(up2[...], l2)).astype(BF)

    @jax.named_scope("key_rows")
    def key_rows(h):
        left = jnp.concatenate([g[384 * h:384 * h + 384, :], up1[...]], axis=1)
        fine[h % 2] = dot(left, jnp.concatenate([qv[...], mid[96 * h:96 * h + 96, :]], axis=0))

    def key_tiles(h):
        for t in range(8):
            for p in range(2):
                for r in range(2):
                    at, to = 192 * r + 24 * t + 12 * p, 24 * (h % 2) + 12 * r
                    kt[h // 2, p, t, to:to + 12, :] = fine[h % 2, at:at + 12, :]

    def core_send(i):
        flight[i, 0] = send(kt.at[i, 1 - core], c0r.at[i], other_core, 2, group(), c0r.at[i])

    @jax.named_scope("query_chunk")
    def query_chunk(i):
        part = dot(pool_t[...], g[:, 384 * i:384 * i + 384])
        part = jnp.transpose(part)
        for hh in range(2):
            for k in range(8):
                at = 192 * hh + 24 * k
                qt[i, k, 24 * hh:24 * hh + 24, :] = part[at:at + 24, :]

    def along(u):
        return (1, cy, zh) if u < 4 else (0, cx, zl)

    def part_of(u, g_, n, c):
        lanes = slice(128 * c, 128 * c + 128)
        tile = g_ * 4 + n
        if u < 4:
            return kt[u, core, tile, :, lanes]
        return qt[u - 4, tile, :, lanes]

    def mates(u):
        dim, n, _ = along(u)
        flip = n + 1 - 2 * (n % 2)
        mirror = 3 - n
        return ((flip, mirror), (mirror, flip))

    def ring(u, n):
        dim = along(u)[0]
        return device(n if dim == 0 else cx, n if dim == 1 else cy, cz, core)

    def last_mate(u):
        if u < 4:
            return device(cx, cy, (1 - zh) * 2 + zl, core)
        return device(cx, cy, zh * 2 + (1 - zl), core)

    @jax.named_scope("step1")
    def step1(u):
        sem = group()
        for c in range(2):
            first, _ = mates(u)[c]
            flip = first + 1 - 2 * (first % 2)
            beyond = (3 - first) if c == 0 else flip
            for j in range(4):
                n = first if j < 2 else beyond
                s1[u, c, j] = part_of(u, j % 2, n, c).astype(BF)
            flight[u, 1] = send(s1.at[u, c], r1.at[u, c], ring(u, first), 3, sem, r1.at[u])

    @jax.named_scope("step2")
    def step2(u):
        sem = group()
        arrived(flight[u, 1])
        for c in range(2):
            _, second = mates(u)[c]
            for j in range(2):
                s2[u, c, j] = (part_of(u, j, second, c) + r1[u, c, 2 + j].astype(F32)).astype(BF)
            flight[u, 2] = send(s2.at[u, c], r2.at[u, c], ring(u, second), 4, sem, r2.at[u])

    @jax.named_scope("step3")
    def step3(u):
        sem = group()
        _, n, z = along(u)
        arrived(flight[u, 2])
        for c in range(2):
            far = part_of(u, 1 - z, n, c) + r1[u, c, 1 - z].astype(F32) + r2[u, c, 1 - z].astype(F32)
            s3[u, c] = far.astype(BF)
            flight[u, 3] = send(s3.at[u, c], r3.at[u, c], last_mate(u), 5, sem, r3.at[u])

    @jax.named_scope("finish")
    def finish(u):
        _, n, z = along(u)
        s = 3 if u < 4 else 2
        at = 48 * (u % 4)
        arrived(flight[u, 3])
        for c in range(2):
            total = part_of(u, z, n, c) + r1[u, c, z].astype(F32) + r2[u, c, z].astype(F32)
            total = (total + r3[u, c].astype(F32)) * 0.0625
            stage[s, at:at + 48, 128 * c:128 * c + 128] = total.astype(BF)

    @jax.named_scope("direct")
    def direct():
        n = group()
        for k in range(8):
            d0s[k] = qt[3, k].astype(BF)
        for dz in range(2):
            for dx in range(4):
                if dz + dx:
                    z, x = (zl + dz) % 2, (cx + dx) % 4
                    flight[7, 1] = send(
                        d0s.at[z * 4 + x], d0r.at[dz * 4 + dx - 1], device(x, cy, zh * 2 + z, core), 12, n, d0r
                    )

    @jax.named_scope("direct_finish")
    def direct_finish():
        arrived(flight[7, 1])
        total = qt[3, zl * 4 + cx]
        for k in range(7):
            total = total + d0r[k].astype(F32)
        stage[2, 144:192, :] = (total * 0.0625).astype(BF)

    @jax.named_scope("core_step")
    def core_step(u):
        arrived(flight[u, 0])
        kt[u, core] = kt[u, core] + c0r[u]
        step1(u)

    @jax.named_scope("image_windows")
    def image_windows(s):
        padt[s] = dot_nt(eye[...], padded(s)).astype(BF)
        v = col(192)
        if s == 0:
            i = div(v, 24)
            f = i * 26 + (v - i * 24)
        else:
            j = div(v, 12)
            f = (v - j * 12) * 18 + j
        for rs in range(3):
            for cs in range(3):
                sel = select(f + tap_offset(s, rs, cs), QP)
                win_t[s, rs * 3 + cs] = dot_nt(padt[s], sel).astype(BF)

    @jax.named_scope("weight_part")
    def weight_part(s, first):
        for t in range(9):
            term = dot(win_t[s, t], stage[s + 2, 0:192, :])
            j, k = t // 3, t % 3
            for h in range(2):
                half = term[:, 128 * h:128 * h + 128]
                rows = slice(256 * k, 256 * k + 256)
                wacc[h, j, rows] = half if first else wacc[h, j, rows] + half
            if not first and k == 2:
                f0.append(send(wacc.at[1 - core, j], a0r.at[j], other_core, 6, group(), a0r.at[j]))

    @jax.named_scope("input_grad")
    def input_grad(s, slot):
        pad = padded(s)
        v = col(192)
        if s == 2:
            i = div(v, 24)
            f = i * 26 + (v - i * 24)
        else:
            f = lax.shift_right_logical(v, 4) * 18 + (v & 15)
        acc = jnp.zeros((192, 256), F32)
        for rs in range(3):
            for cs in range(3):
                sel = select(f + tap_offset(s, 2 - rs, 2 - cs), QP)
                win = dot(sel, pad).astype(BF)
                at = 256 * (rs * 3 + cs)
                acc = acc + dot_nt(win, cw[at:at + 256, :])
        ogs[slot] = acc.astype(BF)

    f0 = []
    tables()
    ld_k.wait()
    pool_keys()
    ld_q.wait()
    ld_gc.wait()
    coarse_levels()
    ld_g[0].wait()
    key_rows(0)
    key_rows(1)
    key_tiles(0)
    ld_g[1].wait()
    key_rows(2)
    key_tiles(1)
    for c in ld_img:
        c.wait()
    pl.semaphore_wait(barrier, len(partners))
    core_send(0)
    hc = [halo_cols(0), halo_cols(1)]
    key_rows(3)
    key_tiles(2)
    ld_g[2].wait()
    key_rows(4)
    key_tiles(3)
    core_send(1)
    core_step(0)
    key_rows(5)
    key_tiles(4)
    ld_g[3].wait()
    key_rows(6)
    key_tiles(5)
    core_send(2)
    core_step(1)

    def queries(i):
        query_chunk(i)
        step1(4 + i)

    queries(0)
    core_step(2)
    step2(0)
    key_rows(7)
    key_tiles(6)
    key_tiles(7)
    core_send(3)
    hr = []
    for s in range(2):
        arrived(hc[s])
        hr.append(halo_rows(s))
    queries(1)
    step2(1)
    core_step(3)
    step3(0)
    queries(2)
    step2(2)
    step2(4)
    query_chunk(3)
    direct()
    step2(5)
    step2(3)
    step3(1)
    arrived(hr[1])
    image_windows(1)
    step2(6)
    step3(2)
    step3(4)
    arrived(hr[0])
    image_windows(0)
    step3(3)
    step3(5)
    step3(6)
    for u in range(4):
        finish(u)
    hk = halo_cols(3)
    weight_part(1, True)
    for u in range(4, 7):
        finish(u)
    direct_finish()
    hq = halo_cols(2)
    weight_part(0, False)

    coords = (cx, cy, cz)
    f1 = []
    for j in range(3):
        arrived(f0[j])
        n = coords[j]
        wacc[core, j] = wacc[core, j] + a0r[j]
        for k in range(4):
            a1s[j, k] = wacc[core, j, 192 * k:192 * k + 192].astype(BF)
        sem = group()
        for d in (1, 2, 3):
            last = send(a1s.at[j, (n + d) % 4], a1r.at[j, d - 1], shift(j, d), 7, sem, a1r.at[j])
        f1.append(last)
    arrived(hk)
    hk = halo_rows(3)
    ld_cw.wait()
    f2 = []
    for j in range(3):
        arrived(f1[j])
        x = wacc[core, j, pl.ds(pl.multiple_of(192 * coords[j], 192), 192), :]
        for d in range(3):
            x = x + a1r[j, d].astype(F32)
        a2[j, 0] = x.astype(BF)
        sem = group()
        for d in (1, 2, 3):
            last = send(a2.at[j, 0], a2.at[j, d], shift((j + 1) % 3, d), 8, sem, a2.at[j, pl.ds(1, 3)])
        f2.append(last)
    arrived(hq)
    hq = halo_rows(2)
    arrived(hk)
    input_grad(3, 1)

    def ring_sum(ref, n):
        y = ref[n].astype(F32)
        for k in (1, 2, 3):
            y = y + ref[(n + 4 - k) % 4].astype(F32)
        return y.astype(BF)

    f3 = []
    for j in range(3):
        arrived(f2[j])
        a3[j, 0] = ring_sum(a2.at[j], coords[(j + 1) % 3])
        sem = group()
        for d in (1, 2, 3):
            last = send(a3.at[j, 0], a3.at[j, d], shift((j + 2) % 3, d), 9, sem, a3.at[j, pl.ds(1, 3)])
        f3.append(last)
    arrived(hq)
    input_grad(2, 0)
    copies = [load(ogs, og_out)]
    f5 = []
    own = []
    for j in range(3):
        arrived(f3[j])
        a4[j] = ring_sum(a3.at[j], coords[(j + 2) % 3])
        mine = w_out.at[core, j, coords[j]]
        sem = group()
        for d in (1, 2, 3):
            last = send(a4.at[j], mine, shift(j, d), 10, sem, a1r.at[j])
        f5.append(last)
        own.append(load(a4.at[j], mine))
    f6 = []
    for j in range(3):
        arrived(f5[j])
        own[j].wait()
        mine = w_out.at[core, j]
        f6.append(send(mine, mine, other_core, 11, group(), mine))
    for j in range(3):
        arrived(f6[j])
    sent = (colp, rowp, c0r, s1, s2, s3, a0r, a1r, a1r, a1r, a1r, a1s, d0r)
    for k, ref in enumerate(sent):
        pltpu.make_async_copy(ref, ref, send_sem.at[k]).wait()
    copies[0].wait()


def widen(og, w, qg_out, kg_out, w_out, wide, sem):
    copies = [
        pltpu.make_async_copy(og.at[0], qg_out, sem.at[0]),
        pltpu.make_async_copy(og.at[1], kg_out, sem.at[1]),
    ]
    for k in range(6):
        rows = pl.ds(384 * k, 384)
        for h in range(2):
            wide[384 * k:384 * k + 384, 128 * h:128 * h + 128] = w[h, 384 * k:384 * k + 384, :].astype(F32)
        copies.append(pltpu.make_async_copy(wide.at[rows], w_out.at[rows], sem.at[2 + k]))
        if k == 0:
            copies[0].start()
            copies[1].start()
        copies[-1].start()
    for c in copies:
        c.wait()


def vmem(*shape, dtype=BF):
    return pltpu.VMEM(shape, dtype)


def body(query_features, key_features, pyramid_grad, query_image, key_image, conv_weight):
    cells = jnp.transpose(pyramid_grad.reshape(QN, CELLS))
    anywhere = pl.BlockSpec(memory_space=pl.ANY)
    og, w = pl.pallas_call(
        kernel,
        out_shape=(
            jax.ShapeDtypeStruct((2, 192, 256), BF),
            jax.ShapeDtypeStruct((2, 3, 4, 192, 128), BF),
        ),
        in_specs=[pl.BlockSpec(memory_space=pltpu.HBM)] * 6,
        out_specs=[pl.BlockSpec(memory_space=pl.ANY)] * 2,
        scratch_shapes=[
            vmem(4096, QN), vmem(QN, 256), vmem(3072, 256), vmem(2304, 256),
            vmem(4096, 256), vmem(256, 4096), vmem(768, 256), vmem(2, 384, 256, dtype=F32),
            vmem(4, 2, 8, 48, 256, dtype=F32), vmem(4, 8, 48, 256, dtype=F32),
            vmem(4, 8, 48, 256, dtype=F32),
            vmem(7, 2, 4, 48, 128), vmem(7, 2, 4, 48, 128),
            vmem(7, 2, 2, 48, 128), vmem(7, 2, 2, 48, 128),
            vmem(7, 2, 48, 128), vmem(7, 2, 48, 128),
            vmem(8, 48, 256), vmem(7, 48, 256),
            vmem(256, 256), vmem(256, 256), vmem(128, 512), vmem(64, 1024), vmem(48, 3072),
            vmem(192, 48), vmem(768, 192), vmem(384, 96),
            vmem(4, ST, 256), vmem(4, 32, 256), vmem(4, 64, 256),
            vmem(2, 256, QP), vmem(2, 9, 256, 192), vmem(2, 3, 768, 128, dtype=F32),
            vmem(3, 768, 128, dtype=F32),
            vmem(3, 4, 192, 128), vmem(3, 3, 192, 128),
            vmem(3, 4, 192, 128), vmem(3, 4, 192, 128), vmem(3, 192, 128), vmem(2, 192, 256),
            pltpu.SemaphoreType.DMA((14,)),
            pltpu.SemaphoreType.DMA((13,)),
            pltpu.SemaphoreType.DMA((52,)),
        ],
        compiler_params=pltpu.CompilerParams(
            collective_id=0, has_side_effects=True, vmem_limit_bytes=VMEM_BYTES
        ),
    )(
        *[
            pltpu.with_memory_space_constraint(x, pltpu.HBM)
            for x in (
                cells,
                query_features.reshape(QN, 256),
                key_features.reshape(3072, 256),
                query_image.reshape(192, 256),
                key_image.reshape(192, 256),
                conv_weight.reshape(2304, 256),
            )
        ]
    )
    qg, kg, w = pl.pallas_call(
        widen,
        out_shape=(
            jax.ShapeDtypeStruct((192, 256), BF),
            jax.ShapeDtypeStruct((192, 256), BF),
            jax.ShapeDtypeStruct((2304, 256), F32),
        ),
        in_specs=[pl.BlockSpec(memory_space=pltpu.VMEM)] * 2,
        out_specs=[pl.BlockSpec(memory_space=pltpu.HBM)] * 3,
        scratch_shapes=[vmem(2304, 256, dtype=F32), pltpu.SemaphoreType.DMA((8,))],
        compiler_params=pltpu.CompilerParams(vmem_limit_bytes=16 * 1024 * 1024),
    )(og, w.reshape(2, 2304, 128))
    return qg.reshape(8, 24, 256), kg.reshape(12, 16, 256), w.reshape(3, 3, 256, 256)


def solution(mesh):
    placed = (
        P("pb", None, None),
        P(None, "ka", None),
        P("pb", "ka", None),
        P("pb", "ka", None),
        P("pb", "ka", None),
        P(),
    )
    return jax.shard_map(
        body,
        mesh=mesh,
        in_specs=placed,
        out_specs=(P("pb", "ka", None), P("pb", "ka", None), P()),
        check_vma=False,
    )
```

```python
import jax
import jax.numpy as jnp
from jax import lax
from jax.experimental import pallas as pl
from jax.experimental.pallas import tpu as pltpu
from jax.sharding import PartitionSpec as P

BF = jnp.bfloat16
F32 = jnp.float32
MESH = pl.DeviceIdType.MESH
CELLS = 4080
QN = 1536
VMEM_BYTES = 50 * 1024 * 1024
QP = 384
ST = 384
NT = (((1,), (1,)), ((), ()))


def dot(a, b):
    return jnp.dot(a, b, preferred_element_type=F32)


def dot_nt(a, b):
    return lax.dot_general(a, b, NT, preferred_element_type=F32)


def div(v, d):
    return lax.shift_right_logical(v * (-(-(1 << 20) // d)), 20)


def col(n):
    return lax.broadcasted_iota(jnp.int32, (n, 1), 0)


def row(n):
    return lax.broadcasted_iota(jnp.int32, (1, n), 1)


def select(src, n, value=1.0):
    wide = lax.broadcasted_iota(jnp.int32, (src.shape[0], n), 1)
    return jnp.where(wide == src, value, 0.0).astype(BF)


def pick(key, n, value):
    tall = lax.broadcasted_iota(jnp.int32, (n, key.shape[1]), 0)
    return jnp.where(tall == key, value, 0.0).astype(BF)


def kernel(
    g_hbm, q_hbm, k_hbm, qi_hbm, ki_hbm, cw_hbm,
    og_out, w_out,
    g, qv, kv, cw, pool, pool_t, mid, fine, kt, qt,
    c0r, s1, r1, s2, r2, s3, r3, d0s, d0r,
    eye, perm, mean1, mean2, mean3, up3, up2, up1,
    stage, colp, rowp, padt, win_t, wacc,
    a0r, a1s, a1r, a2, a3, a4, ogs,
    in_sem, send_sem, recv_sem,
):
    pb, ka = lax.axis_index("pb"), lax.axis_index("ka")
    core = pb % 2
    cy = (pb // 2) % 4
    zh = pb // 8
    cx = ka % 4
    zl = ka // 4
    cz = zh * 2 + zl

    def device(x, y, z, c):
        return {"pb": ((z // 2) * 4 + y) * 2 + c, "ka": (z % 2) * 4 + x}

    def shift(dim, d):
        return device(
            (cx + d) % 4 if dim == 0 else cx,
            (cy + d) % 4 if dim == 1 else cy,
            (cz + d) % 4 if dim == 2 else cz,
            core,
        )

    other_core = device(cx, cy, cz, 1 - core)
    pb_up = {"pb": (pb + 15) % 16, "ka": ka}
    pb_down = {"pb": (pb + 1) % 16, "ka": ka}
    ka_up = {"pb": pb, "ka": (ka + 7) % 8}
    ka_down = {"pb": pb, "ka": (ka + 1) % 8}

    loads = []
    used = [0]

    def group():
        used[0] += 1
        return used[0] - 1

    def send(src, dst, dev, k, n, whole):
        pltpu.make_async_remote_copy(
            src_ref=src, dst_ref=dst, send_sem=send_sem.at[k], recv_sem=recv_sem.at[n],
            device_id=dev, device_id_type=MESH,
        ).start()
        return whole, n

    def arrived(item):
        whole, n = item
        pltpu.make_async_copy(whole, whole, recv_sem.at[n]).wait()

    def load(src, dst):
        copy = pltpu.make_async_copy(src, dst, in_sem.at[len(loads)])
        copy.start()
        loads.append(copy)
        return copy

    ld_k = [load(k_hbm.at[pl.ds(1024 * i, 1024)], kv.at[pl.ds(1024 * i, 1024)]) for i in range(3)]
    ld_q = load(q_hbm, qv)
    ld_gc = load(g_hbm.at[pl.ds(3072, 1008)], g.at[pl.ds(3072, 1008)])
    ld_img = [load(qi_hbm, stage.at[0, pl.ds(0, 192)]), load(ki_hbm, stage.at[1, pl.ds(0, 192)])]
    ld_g = [load(g_hbm.at[pl.ds(768 * i, 768)], g.at[pl.ds(768 * i, 768)]) for i in range(4)]
    ld_cw = load(cw_hbm, cw)

    barrier = pltpu.get_barrier_semaphore()
    partners = [other_core, pb_up, pb_down, ka_up, ka_down]
    partners += [shift(dim, d) for dim in range(3) for d in (1, 2, 3)]
    for partner in partners:
        pl.semaphore_signal(barrier, inc=1, device_id=partner, device_id_type=MESH)

    for s in range(4):
        stage[s, 288:ST, :] = jnp.zeros((ST - 288, 256), BF)
    g[CELLS:4096, :] = jnp.zeros((4096 - CELLS, QN), BF)
    pool[CELLS:4096, :] = jnp.zeros((4096 - CELLS, 256), BF)

    rows_of = (8, 12, 8, 12)
    cols_of = (24, 16, 24, 16)

    def tile_index(s, i, j):
        return j * 12 + i if s == 3 else i * cols_of[s] + j

    @jax.named_scope("halo_cols")
    def halo_cols(s):
        n_r, n_c = rows_of[s], cols_of[s]
        v = col(32)
        i = v & 15
        src = jnp.where(v < 16, tile_index(s, i, 0), tile_index(s, i, n_c - 1))
        src = jnp.where(i < n_r, src, -1)
        colp[s] = dot(select(src, 192), stage[s, 0:192, :]).astype(BF)
        n = group()
        whole = stage.at[s, pl.ds(192, 32)]
        send(colp.at[s, pl.ds(0, 16)], stage.at[s, pl.ds(208, 16)], ka_up, 0, n, whole)
        return send(colp.at[s, pl.ds(16, 16)], stage.at[s, pl.ds(192, 16)], ka_down, 0, n, whole)

    @jax.named_scope("halo_rows")
    def halo_rows(s):
        n_r, n_c = rows_of[s], cols_of[s]
        v = col(64)
        j = (v & 31) - 1
        i = jnp.where(v < 32, 0, n_r - 1)
        src = tile_index(s, i, j)
        src = jnp.where(j < 0, jnp.where(ka == 0, -1, 192 + i), src)
        src = jnp.where(j == n_c, jnp.where(ka == 7, -1, 208 + i), src)
        src = jnp.where(j > n_c, -1, src)
        rowp[s] = dot(select(src, 224), stage[s, 0:224, :]).astype(BF)
        n = group()
        whole = stage.at[s, pl.ds(224, 64)]
        send(rowp.at[s, pl.ds(0, 32)], stage.at[s, pl.ds(256, 32)], pb_up, 1, n, whole)
        return send(rowp.at[s, pl.ds(32, 32)], stage.at[s, pl.ds(224, 32)], pb_down, 1, n, whole)

    def padded(s):
        n_r, n_c = rows_of[s], cols_of[s]
        v = col(QP)
        ip = div(v, n_c + 2)
        jp = v - ip * (n_c + 2)
        i, j = ip - 1, jp - 1
        src = tile_index(s, i, j)
        src = jnp.where(j < 0, jnp.where(ka == 0, -1, 192 + i), src)
        src = jnp.where(j == n_c, jnp.where(ka == 7, -1, 208 + i), src)
        src = jnp.where(i < 0, jnp.where(pb == 0, -1, 224 + jp), src)
        src = jnp.where(i == n_r, jnp.where(pb == 15, -1, 256 + jp), src)
        src = jnp.where(i > n_r, -1, src)
        return dot(select(src, ST), stage[s]).astype(BF)

    def tap_offset(s, rs, cs):
        pitch = cols_of[s] + 2
        return cs * pitch + rs if s % 2 else rs * pitch + cs

    flight = {}

    @jax.named_scope("tables")
    def tables():
        o = col(256)
        eye[...] = select(o, 256)
        perm[...] = select((o & 15) * 16 + lax.shift_right_logical(o, 4), 256)
        k = row(512)
        mean1[...] = pick(lax.shift_right_logical(k & 15, 1) * 16 + lax.shift_right_logical(k, 5), 128, 0.25)
        k = row(1024)
        mean2[...] = pick(lax.shift_right_logical(k & 15, 2) * 16 + lax.shift_right_logical(k, 6), 64, 0.0625)
        k = row(3072)
        key = (lax.shift_right_logical(k, 3) & 1) * 24 + lax.shift_right_logical(k, 7)
        mean3[...] = pick(key, 48, 0.015625)
        v = col(192)
        r = div(v, 48)
        up3[...] = select(lax.shift_right_logical(r, 1) * 24 + lax.shift_right_logical(v - r * 48, 1), 48)
        v = col(768)
        r = div(v, 96)
        up2[...] = select(lax.shift_right_logical(r, 1) * 48 + lax.shift_right_logical(v - r * 96, 1), 192)
        r = div(v, 192)
        up1[...] = select(lax.shift_right_logical(r, 1) * 96 + lax.shift_right_logical(v - r * 192, 1), 192)

    @jax.named_scope("pool_keys")
    def pool_keys():
        for b in range(12):
            if b % 4 == 0:
                ld_k[b // 4].wait()
            block = dot(perm[...], kv[256 * b:256 * b + 256, :]).astype(BF)
            for r in range(16):
                pool[192 * r + 16 * b:192 * r + 16 * b + 16, :] = block[16 * r:16 * r + 16, :]
        for b in range(6):
            block = dot(mean1[...], kv[512 * b:512 * b + 512, :]).astype(BF)
            for r in range(8):
                at = 3072 + 96 * r + 16 * b
                pool[at:at + 16, :] = block[16 * r:16 * r + 16, :]
        for b in range(3):
            block = dot(mean2[...], kv[1024 * b:1024 * b + 1024, :]).astype(BF)
            for r in range(4):
                at = 3840 + 48 * r + 16 * b
                pool[at:at + 16, :] = block[16 * r:16 * r + 16, :]
        pool[4032:4080, :] = dot(mean3[...], kv[...]).astype(BF)
        for b in range(16):
            pool_t[:, 256 * b:256 * b + 256] = dot_nt(eye[...], pool[256 * b:256 * b + 256, :]).astype(BF)

    @jax.named_scope("coarse_levels")
    def coarse_levels():
        l3 = (dot(g[4032:4080, :], qv[...]) * (1.0 / 64.0)).astype(BF)
        l2 = (dot(g[3840:4032, :], qv[...]) * (1.0 / 16.0) + dot(up3[...], l3)).astype(BF)
        for k in range(3):
            at = 256 * k
            part = dot(g[3072 + at:3328 + at, :], qv[...]) * 0.25 + dot(up2[at:at + 256, :], l2)
            mid[at:at + 256, :] = part.astype(BF)

    @jax.named_scope("key_rows")
    def key_rows(i):
        right = jnp.concatenate([qv[...], mid[192 * i:192 * i + 192, :]], axis=0)
        for k in range(3):
            at = 768 * i + 256 * k
            left = jnp.concatenate([g[at:at + 256, :], up1[256 * k:256 * k + 256, :]], axis=1)
            fine[i % 2, 256 * k:256 * k + 256, :] = dot(left, right)

    def key_tiles(i):
        for t in range(8):
            for p in range(2):
                for r in range(4):
                    at = 192 * r + 24 * t + 12 * p
                    kt[i, p, t, 12 * r:12 * r + 12, :] = fine[i % 2, at:at + 12, :]

    def core_send(i):
        flight[i, 0] = send(kt.at[i, 1 - core], c0r.at[i], other_core, 2, group(), c0r.at[i])

    @jax.named_scope("query_chunk")
    def query_chunk(i):
        part = dot(pool_t[...], g[:, 384 * i:384 * i + 384])
        part = jnp.transpose(part)
        for hh in range(2):
            for k in range(8):
                at = 192 * hh + 24 * k
                qt[i, k, 24 * hh:24 * hh + 24, :] = part[at:at + 24, :]

    def along(u):
        return (1, cy, zh) if u < 4 else (0, cx, zl)

    def part_of(u, g_, n, c):
        lanes = slice(128 * c, 128 * c + 128)
        tile = g_ * 4 + n
        if u < 4:
            return kt[u, core, tile, :, lanes]
        return qt[u - 4, tile, :, lanes]

    def mates(u):
        dim, n, _ = along(u)
        flip = n + 1 - 2 * (n % 2)
        mirror = 3 - n
        return ((flip, mirror), (mirror, flip))

    def ring(u, n):
        dim = along(u)[0]
        return device(n if dim == 0 else cx, n if dim == 1 else cy, cz, core)

    def last_mate(u):
        if u < 4:
            return device(cx, cy, (1 - zh) * 2 + zl, core)
        return device(cx, cy, zh * 2 + (1 - zl), core)

    @jax.named_scope("step1")
    def step1(u):
        sem = group()
        for c in range(2):
            first, _ = mates(u)[c]
            flip = first + 1 - 2 * (first % 2)
            beyond = (3 - first) if c == 0 else flip
            for j in range(4):
                n = first if j < 2 else beyond
                s1[u, c, j] = part_of(u, j % 2, n, c).astype(BF)
            flight[u, 1] = send(s1.at[u, c], r1.at[u, c], ring(u, first), 3, sem, r1.at[u])

    @jax.named_scope("step2")
    def step2(u):
        sem = group()
        arrived(flight[u, 1])
        for c in range(2):
            _, second = mates(u)[c]
            for j in range(2):
                s2[u, c, j] = (part_of(u, j, second, c) + r1[u, c, 2 + j].astype(F32)).astype(BF)
            flight[u, 2] = send(s2.at[u, c], r2.at[u, c], ring(u, second), 4, sem, r2.at[u])

    @jax.named_scope("step3")
    def step3(u):
        sem = group()
        _, n, z = along(u)
        arrived(flight[u, 2])
        for c in range(2):
            far = part_of(u, 1 - z, n, c) + r1[u, c, 1 - z].astype(F32) + r2[u, c, 1 - z].astype(F32)
            s3[u, c] = far.astype(BF)
            flight[u, 3] = send(s3.at[u, c], r3.at[u, c], last_mate(u), 5, sem, r3.at[u])

    @jax.named_scope("finish")
    def finish(u):
        _, n, z = along(u)
        s = 3 if u < 4 else 2
        at = 48 * (u % 4)
        arrived(flight[u, 3])
        for c in range(2):
            total = part_of(u, z, n, c) + r1[u, c, z].astype(F32) + r2[u, c, z].astype(F32)
            total = (total + r3[u, c].astype(F32)) * 0.0625
            stage[s, at:at + 48, 128 * c:128 * c + 128] = total.astype(BF)

    @jax.named_scope("direct")
    def direct():
        n = group()
        for k in range(8):
            d0s[k] = qt[3, k].astype(BF)
        for dz in range(2):
            for dx in range(4):
                if dz + dx:
                    z, x = (zl + dz) % 2, (cx + dx) % 4
                    flight[7, 1] = send(
                        d0s.at[z * 4 + x], d0r.at[dz * 4 + dx - 1], device(x, cy, zh * 2 + z, core), 12, n, d0r
                    )

    @jax.named_scope("direct_finish")
    def direct_finish():
        arrived(flight[7, 1])
        total = qt[3, zl * 4 + cx]
        for k in range(7):
            total = total + d0r[k].astype(F32)
        stage[2, 144:192, :] = (total * 0.0625).astype(BF)

    @jax.named_scope("core_step")
    def core_step(u):
        arrived(flight[u, 0])
        kt[u, core] = kt[u, core] + c0r[u]
        step1(u)

    @jax.named_scope("image_windows")
    def image_windows(s):
        padt[s] = dot_nt(eye[...], padded(s)).astype(BF)
        v = col(192)
        if s == 0:
            i = div(v, 24)
            f = i * 26 + (v - i * 24)
        else:
            j = div(v, 12)
            f = (v - j * 12) * 18 + j
        for rs in range(3):
            for cs in range(3):
                sel = select(f + tap_offset(s, rs, cs), QP)
                win_t[s, rs * 3 + cs] = dot_nt(padt[s], sel).astype(BF)

    @jax.named_scope("weight_part")
    def weight_part(s, first):
        for t in range(9):
            term = dot(win_t[s, t], stage[s + 2, 0:192, :])
            j, k = t // 3, t % 3
            for h in range(2):
                half = term[:, 128 * h:128 * h + 128]
                rows = slice(256 * k, 256 * k + 256)
                wacc[h, j, rows] = half if first else wacc[h, j, rows] + half
            if not first and k == 2:
                f0.append(send(wacc.at[1 - core, j], a0r.at[j], other_core, 6, group(), a0r.at[j]))

    @jax.named_scope("input_grad")
    def input_grad(s, slot):
        pad = padded(s)
        v = col(192)
        if s == 2:
            i = div(v, 24)
            f = i * 26 + (v - i * 24)
        else:
            f = lax.shift_right_logical(v, 4) * 18 + (v & 15)
        acc = jnp.zeros((192, 256), F32)
        for rs in range(3):
            for cs in range(3):
                sel = select(f + tap_offset(s, 2 - rs, 2 - cs), QP)
                win = dot(sel, pad).astype(BF)
                at = 256 * (rs * 3 + cs)
                acc = acc + dot_nt(win, cw[at:at + 256, :])
        ogs[slot] = acc.astype(BF)

    f0 = []
    tables()
    pool_keys()
    ld_q.wait()
    ld_gc.wait()
    coarse_levels()
    ld_g[0].wait()
    key_rows(0)
    key_tiles(0)
    for c in ld_img:
        c.wait()
    pl.semaphore_wait(barrier, len(partners))
    core_send(0)
    hc = [halo_cols(0), halo_cols(1)]

    def keys(i):
        if i < 3:
            ld_g[i].wait()
        key_rows(i)
        key_tiles(i)
        core_send(i)

    keys(1)
    core_step(0)
    keys(2)
    core_step(1)
    ld_g[3].wait()

    def queries(i):
        query_chunk(i)
        step1(4 + i)

    queries(0)
    core_step(2)
    step2(0)
    keys(3)
    hr = []
    for s in range(2):
        arrived(hc[s])
        hr.append(halo_rows(s))
    queries(1)
    step2(1)
    core_step(3)
    queries(2)
    step3(0)
    step2(2)
    step2(4)
    query_chunk(3)
    direct()
    step2(5)
    step2(3)
    step3(1)
    arrived(hr[1])
    image_windows(1)
    step2(6)
    step3(2)
    step3(4)
    arrived(hr[0])
    image_windows(0)
    step3(3)
    step3(5)
    step3(6)
    for u in range(4):
        finish(u)
    hk = halo_cols(3)
    weight_part(1, True)
    for u in range(4, 7):
        finish(u)
    direct_finish()
    hq = halo_cols(2)
    weight_part(0, False)

    coords = (cx, cy, cz)
    f1 = []
    for j in range(3):
        arrived(f0[j])
        n = coords[j]
        wacc[core, j] = wacc[core, j] + a0r[j]
        for k in range(4):
            a1s[j, k] = wacc[core, j, 192 * k:192 * k + 192].astype(BF)
        sem = group()
        for d in (1, 2, 3):
            last = send(a1s.at[j, (n + d) % 4], a1r.at[j, d - 1], shift(j, d), 7, sem, a1r.at[j])
        f1.append(last)
    arrived(hk)
    hk = halo_rows(3)
    ld_cw.wait()
    f2 = []
    for j in range(3):
        arrived(f1[j])
        x = wacc[core, j, pl.ds(pl.multiple_of(192 * coords[j], 192), 192), :]
        for d in range(3):
            x = x + a1r[j, d].astype(F32)
        a2[j, 0] = x.astype(BF)
        sem = group()
        for d in (1, 2, 3):
            last = send(a2.at[j, 0], a2.at[j, d], shift((j + 1) % 3, d), 8, sem, a2.at[j, pl.ds(1, 3)])
        f2.append(last)
    arrived(hq)
    hq = halo_rows(2)
    arrived(hk)
    input_grad(3, 1)

    def ring_sum(ref, n):
        y = ref[n].astype(F32)
        for k in (1, 2, 3):
            y = y + ref[(n + 4 - k) % 4].astype(F32)
        return y.astype(BF)

    f3 = []
    for j in range(3):
        arrived(f2[j])
        a3[j, 0] = ring_sum(a2.at[j], coords[(j + 1) % 3])
        sem = group()
        for d in (1, 2, 3):
            last = send(a3.at[j, 0], a3.at[j, d], shift((j + 2) % 3, d), 9, sem, a3.at[j, pl.ds(1, 3)])
        f3.append(last)
    arrived(hq)
    input_grad(2, 0)
    copies = [load(ogs, og_out)]
    f5 = []
    own = []
    for j in range(3):
        arrived(f3[j])
        a4[j] = ring_sum(a3.at[j], coords[(j + 2) % 3])
        mine = w_out.at[core, j, coords[j]]
        sem = group()
        for d in (1, 2, 3):
            last = send(a4.at[j], mine, shift(j, d), 10, sem, a1r.at[j])
        f5.append(last)
        own.append(load(a4.at[j], mine))
    f6 = []
    for j in range(3):
        arrived(f5[j])
        own[j].wait()
        mine = w_out.at[core, j]
        f6.append(send(mine, mine, other_core, 11, group(), mine))
    for j in range(3):
        arrived(f6[j])
    sent = (colp, rowp, c0r, s1, s2, s3, a0r, a1r, a1r, a1r, a1r, a1s, d0r)
    for k, ref in enumerate(sent):
        pltpu.make_async_copy(ref, ref, send_sem.at[k]).wait()
    copies[0].wait()


def widen(og, w, qg_out, kg_out, w_out, wide, sem):
    copies = [
        pltpu.make_async_copy(og.at[0], qg_out, sem.at[0]),
        pltpu.make_async_copy(og.at[1], kg_out, sem.at[1]),
    ]
    for k in range(6):
        rows = pl.ds(384 * k, 384)
        for h in range(2):
            wide[384 * k:384 * k + 384, 128 * h:128 * h + 128] = w[h, 384 * k:384 * k + 384, :].astype(F32)
        copies.append(pltpu.make_async_copy(wide.at[rows], w_out.at[rows], sem.at[2 + k]))
        if k == 0:
            copies[0].start()
            copies[1].start()
        copies[-1].start()
    for c in copies:
        c.wait()


def vmem(*shape, dtype=BF):
    return pltpu.VMEM(shape, dtype)


def body(query_features, key_features, pyramid_grad, query_image, key_image, conv_weight):
    cells = jnp.transpose(pyramid_grad.reshape(QN, CELLS))
    anywhere = pl.BlockSpec(memory_space=pl.ANY)
    og, w = pl.pallas_call(
        kernel,
        out_shape=(
            jax.ShapeDtypeStruct((2, 192, 256), BF),
            jax.ShapeDtypeStruct((2, 3, 4, 192, 128), BF),
        ),
        in_specs=[pl.BlockSpec(memory_space=pltpu.HBM)] * 6,
        out_specs=[pl.BlockSpec(memory_space=pl.ANY)] * 2,
        scratch_shapes=[
            vmem(4096, QN), vmem(QN, 256), vmem(3072, 256), vmem(2304, 256),
            vmem(4096, 256), vmem(256, 4096), vmem(768, 256), vmem(2, 768, 256, dtype=F32),
            vmem(4, 2, 8, 48, 256, dtype=F32), vmem(4, 8, 48, 256, dtype=F32),
            vmem(4, 8, 48, 256, dtype=F32),
            vmem(7, 2, 4, 48, 128), vmem(7, 2, 4, 48, 128),
            vmem(7, 2, 2, 48, 128), vmem(7, 2, 2, 48, 128),
            vmem(7, 2, 48, 128), vmem(7, 2, 48, 128),
            vmem(8, 48, 256), vmem(7, 48, 256),
            vmem(256, 256), vmem(256, 256), vmem(128, 512), vmem(64, 1024), vmem(48, 3072),
            vmem(192, 48), vmem(768, 192), vmem(768, 192),
            vmem(4, ST, 256), vmem(4, 32, 256), vmem(4, 64, 256),
            vmem(2, 256, QP), vmem(2, 9, 256, 192), vmem(2, 3, 768, 128, dtype=F32),
            vmem(3, 768, 128, dtype=F32),
            vmem(3, 4, 192, 128), vmem(3, 3, 192, 128),
            vmem(3, 4, 192, 128), vmem(3, 4, 192, 128), vmem(3, 192, 128), vmem(2, 192, 256),
            pltpu.SemaphoreType.DMA((16,)),
            pltpu.SemaphoreType.DMA((13,)),
            pltpu.SemaphoreType.DMA((52,)),
        ],
        compiler_params=pltpu.CompilerParams(
            collective_id=0, has_side_effects=True, vmem_limit_bytes=VMEM_BYTES
        ),
    )(
        *[
            pltpu.with_memory_space_constraint(x, pltpu.HBM)
            for x in (
                cells,
                query_features.reshape(QN, 256),
                key_features.reshape(3072, 256),
                query_image.reshape(192, 256),
                key_image.reshape(192, 256),
                conv_weight.reshape(2304, 256),
            )
        ]
    )
    qg, kg, w = pl.pallas_call(
        widen,
        out_shape=(
            jax.ShapeDtypeStruct((192, 256), BF),
            jax.ShapeDtypeStruct((192, 256), BF),
            jax.ShapeDtypeStruct((2304, 256), F32),
        ),
        in_specs=[pl.BlockSpec(memory_space=pltpu.VMEM)] * 2,
        out_specs=[pl.BlockSpec(memory_space=pltpu.HBM)] * 3,
        scratch_shapes=[vmem(2304, 256, dtype=F32), pltpu.SemaphoreType.DMA((8,))],
        compiler_params=pltpu.CompilerParams(vmem_limit_bytes=16 * 1024 * 1024),
    )(og, w.reshape(2, 2304, 128))
    return qg.reshape(8, 24, 256), kg.reshape(12, 16, 256), w.reshape(3, 3, 256, 256)


def solution(mesh):
    placed = (
        P("pb", None, None),
        P(None, "ka", None),
        P("pb", "ka", None),
        P("pb", "ka", None),
        P("pb", "ka", None),
        P(),
    )
    return jax.shard_map(
        body,
        mesh=mesh,
        in_specs=placed,
        out_specs=(P("pb", "ka", None), P("pb", "ka", None), P()),
        check_vma=False,
    )
```

```python
import jax
import jax.numpy as jnp
from jax import lax
from jax.experimental import pallas as pl
from jax.experimental.pallas import tpu as pltpu
from jax.sharding import PartitionSpec as P

BF = jnp.bfloat16
F32 = jnp.float32
MESH = pl.DeviceIdType.MESH
CELLS = 4080
QN = 1536
VMEM_BYTES = 50 * 1024 * 1024
QP = 384
ST = 384
NT = (((1,), (1,)), ((), ()))


def dot(a, b):
    return jnp.dot(a, b, preferred_element_type=F32)


def dot_nt(a, b):
    return lax.dot_general(a, b, NT, preferred_element_type=F32)


def div(v, d):
    return lax.shift_right_logical(v * (-(-(1 << 20) // d)), 20)


def col(n):
    return lax.broadcasted_iota(jnp.int32, (n, 1), 0)


def row(n):
    return lax.broadcasted_iota(jnp.int32, (1, n), 1)


def select(src, n, value=1.0):
    wide = lax.broadcasted_iota(jnp.int32, (src.shape[0], n), 1)
    return jnp.where(wide == src, value, 0.0).astype(BF)


def pick(key, n, value):
    tall = lax.broadcasted_iota(jnp.int32, (n, key.shape[1]), 0)
    return jnp.where(tall == key, value, 0.0).astype(BF)


def kernel(
    g_hbm, q_hbm, k_hbm, qi_hbm, ki_hbm, cw_hbm,
    og_out, w_out,
    g, qv, kv, cw, pool, pool_t, mid, fine, kt, qt,
    c0r, s1, r1, s2, r2, s3, r3, d0s, d0r, e1s, e1r, e2s, e2r,
    eye, perm, mean1, mean2, mean3, up3, up2, up1,
    stage, colp, rowp, padt, win_t, wacc,
    a0r, a1s, a1r, a2, a3, a4, ogs,
    in_sem, send_sem, recv_sem,
):
    pb, ka = lax.axis_index("pb"), lax.axis_index("ka")
    core = pb % 2
    cy = (pb // 2) % 4
    zh = pb // 8
    cx = ka % 4
    zl = ka // 4
    cz = zh * 2 + zl

    def device(x, y, z, c):
        return {"pb": ((z // 2) * 4 + y) * 2 + c, "ka": (z % 2) * 4 + x}

    def shift(dim, d):
        return device(
            (cx + d) % 4 if dim == 0 else cx,
            (cy + d) % 4 if dim == 1 else cy,
            (cz + d) % 4 if dim == 2 else cz,
            core,
        )

    other_core = device(cx, cy, cz, 1 - core)
    pb_up = {"pb": (pb + 15) % 16, "ka": ka}
    pb_down = {"pb": (pb + 1) % 16, "ka": ka}
    ka_up = {"pb": pb, "ka": (ka + 7) % 8}
    ka_down = {"pb": pb, "ka": (ka + 1) % 8}

    loads = []
    used = [0]

    def group():
        used[0] += 1
        return used[0] - 1

    def send(src, dst, dev, k, n, whole):
        pltpu.make_async_remote_copy(
            src_ref=src, dst_ref=dst, send_sem=send_sem.at[k], recv_sem=recv_sem.at[n],
            device_id=dev, device_id_type=MESH,
        ).start()
        return whole, n

    def arrived(item):
        whole, n = item
        pltpu.make_async_copy(whole, whole, recv_sem.at[n]).wait()

    def load(src, dst):
        copy = pltpu.make_async_copy(src, dst, in_sem.at[len(loads)])
        copy.start()
        loads.append(copy)
        return copy

    ld_k = [load(k_hbm.at[pl.ds(1024 * i, 1024)], kv.at[pl.ds(1024 * i, 1024)]) for i in range(3)]
    ld_q = load(q_hbm, qv)
    ld_gc = load(g_hbm.at[pl.ds(3072, 1008)], g.at[pl.ds(3072, 1008)])
    ld_img = [load(qi_hbm, stage.at[0, pl.ds(0, 192)]), load(ki_hbm, stage.at[1, pl.ds(0, 192)])]
    ld_g = [load(g_hbm.at[pl.ds(768 * i, 768)], g.at[pl.ds(768 * i, 768)]) for i in range(4)]
    ld_cw = load(cw_hbm, cw)

    barrier = pltpu.get_barrier_semaphore()
    partners = [other_core, pb_up, pb_down, ka_up, ka_down]
    partners += [shift(dim, d) for dim in range(3) for d in (1, 2, 3)]
    for partner in partners:
        pl.semaphore_signal(barrier, inc=1, device_id=partner, device_id_type=MESH)

    for s in range(4):
        stage[s, 288:ST, :] = jnp.zeros((ST - 288, 256), BF)
    g[CELLS:4096, :] = jnp.zeros((4096 - CELLS, QN), BF)
    pool[CELLS:4096, :] = jnp.zeros((4096 - CELLS, 256), BF)

    rows_of = (8, 12, 8, 12)
    cols_of = (24, 16, 24, 16)

    def tile_index(s, i, j):
        return j * 12 + i if s == 3 else i * cols_of[s] + j

    @jax.named_scope("halo_cols")
    def halo_cols(s):
        n_r, n_c = rows_of[s], cols_of[s]
        v = col(32)
        i = v & 15
        src = jnp.where(v < 16, tile_index(s, i, 0), tile_index(s, i, n_c - 1))
        src = jnp.where(i < n_r, src, -1)
        colp[s] = dot(select(src, 192), stage[s, 0:192, :]).astype(BF)
        n = group()
        whole = stage.at[s, pl.ds(192, 32)]
        send(colp.at[s, pl.ds(0, 16)], stage.at[s, pl.ds(208, 16)], ka_up, 0, n, whole)
        return send(colp.at[s, pl.ds(16, 16)], stage.at[s, pl.ds(192, 16)], ka_down, 0, n, whole)

    @jax.named_scope("halo_rows")
    def halo_rows(s):
        n_r, n_c = rows_of[s], cols_of[s]
        v = col(64)
        j = (v & 31) - 1
        i = jnp.where(v < 32, 0, n_r - 1)
        src = tile_index(s, i, j)
        src = jnp.where(j < 0, jnp.where(ka == 0, -1, 192 + i), src)
        src = jnp.where(j == n_c, jnp.where(ka == 7, -1, 208 + i), src)
        src = jnp.where(j > n_c, -1, src)
        rowp[s] = dot(select(src, 224), stage[s, 0:224, :]).astype(BF)
        n = group()
        whole = stage.at[s, pl.ds(224, 64)]
        send(rowp.at[s, pl.ds(0, 32)], stage.at[s, pl.ds(256, 32)], pb_up, 1, n, whole)
        return send(rowp.at[s, pl.ds(32, 32)], stage.at[s, pl.ds(224, 32)], pb_down, 1, n, whole)

    def padded(s):
        n_r, n_c = rows_of[s], cols_of[s]
        v = col(QP)
        ip = div(v, n_c + 2)
        jp = v - ip * (n_c + 2)
        i, j = ip - 1, jp - 1
        src = tile_index(s, i, j)
        src = jnp.where(j < 0, jnp.where(ka == 0, -1, 192 + i), src)
        src = jnp.where(j == n_c, jnp.where(ka == 7, -1, 208 + i), src)
        src = jnp.where(i < 0, jnp.where(pb == 0, -1, 224 + jp), src)
        src = jnp.where(i == n_r, jnp.where(pb == 15, -1, 256 + jp), src)
        src = jnp.where(i > n_r, -1, src)
        return dot(select(src, ST), stage[s]).astype(BF)

    def tap_offset(s, rs, cs):
        pitch = cols_of[s] + 2
        return cs * pitch + rs if s % 2 else rs * pitch + cs

    flight = {}
    slot = {0: 0, 1: 1, 2: 2, 4: 3, 5: 4}
    place = {3: 0, 6: 1}

    @jax.named_scope("tables")
    def tables():
        o = col(256)
        eye[...] = select(o, 256)
        perm[...] = select((o & 15) * 16 + lax.shift_right_logical(o, 4), 256)
        k = row(512)
        mean1[...] = pick(lax.shift_right_logical(k & 15, 1) * 16 + lax.shift_right_logical(k, 5), 128, 0.25)
        k = row(1024)
        mean2[...] = pick(lax.shift_right_logical(k & 15, 2) * 16 + lax.shift_right_logical(k, 6), 64, 0.0625)
        k = row(3072)
        key = (lax.shift_right_logical(k, 3) & 1) * 24 + lax.shift_right_logical(k, 7)
        mean3[...] = pick(key, 48, 0.015625)
        v = col(192)
        r = div(v, 48)
        up3[...] = select(lax.shift_right_logical(r, 1) * 24 + lax.shift_right_logical(v - r * 48, 1), 48)
        v = col(768)
        r = div(v, 96)
        up2[...] = select(lax.shift_right_logical(r, 1) * 48 + lax.shift_right_logical(v - r * 96, 1), 192)
        r = div(v, 192)
        up1[...] = select(lax.shift_right_logical(r, 1) * 96 + lax.shift_right_logical(v - r * 192, 1), 192)

    @jax.named_scope("pool_keys")
    def pool_keys():
        for b in range(12):
            if b % 4 == 0:
                ld_k[b // 4].wait()
            block = dot(perm[...], kv[256 * b:256 * b + 256, :]).astype(BF)
            for r in range(16):
                pool[192 * r + 16 * b:192 * r + 16 * b + 16, :] = block[16 * r:16 * r + 16, :]
        for b in range(6):
            block = dot(mean1[...], kv[512 * b:512 * b + 512, :]).astype(BF)
            for r in range(8):
                at = 3072 + 96 * r + 16 * b
                pool[at:at + 16, :] = block[16 * r:16 * r + 16, :]
        for b in range(3):
            block = dot(mean2[...], kv[1024 * b:1024 * b + 1024, :]).astype(BF)
            for r in range(4):
                at = 3840 + 48 * r + 16 * b
                pool[at:at + 16, :] = block[16 * r:16 * r + 16, :]
        pool[4032:4080, :] = dot(mean3[...], kv[...]).astype(BF)
        for b in range(16):
            pool_t[:, 256 * b:256 * b + 256] = dot_nt(eye[...], pool[256 * b:256 * b + 256, :]).astype(BF)

    @jax.named_scope("coarse_levels")
    def coarse_levels():
        l3 = (dot(g[4032:4080, :], qv[...]) * (1.0 / 64.0)).astype(BF)
        l2 = (dot(g[3840:4032, :], qv[...]) * (1.0 / 16.0) + dot(up3[...], l3)).astype(BF)
        for k in range(3):
            at = 256 * k
            part = dot(g[3072 + at:3328 + at, :], qv[...]) * 0.25 + dot(up2[at:at + 256, :], l2)
            mid[at:at + 256, :] = part.astype(BF)

    @jax.named_scope("key_rows")
    def key_rows(i):
        right = jnp.concatenate([qv[...], mid[192 * i:192 * i + 192, :]], axis=0)
        for k in range(3):
            at = 768 * i + 256 * k
            left = jnp.concatenate([g[at:at + 256, :], up1[256 * k:256 * k + 256, :]], axis=1)
            fine[i % 2, 256 * k:256 * k + 256, :] = dot(left, right)

    def key_tiles(i):
        for t in range(8):
            for p in range(2):
                for r in range(4):
                    at = 192 * r + 24 * t + 12 * p
                    kt[i, p, t, 12 * r:12 * r + 12, :] = fine[i % 2, at:at + 12, :]

    def core_send(i):
        flight[i, 0] = send(kt.at[i, 1 - core], c0r.at[i], other_core, 2, group(), c0r.at[i])

    @jax.named_scope("query_chunk")
    def query_chunk(i):
        part = dot(pool_t[...], g[:, 384 * i:384 * i + 384])
        part = jnp.transpose(part)
        for hh in range(2):
            for k in range(8):
                at = 192 * hh + 24 * k
                qt[i, k, 24 * hh:24 * hh + 24, :] = part[at:at + 24, :]

    def along(u):
        return (1, cy, zh) if u < 4 else (0, cx, zl)

    def part_of(u, g_, n, c):
        lanes = slice(128 * c, 128 * c + 128)
        tile = g_ * 4 + n
        if u < 4:
            return kt[u, core, tile, :, lanes]
        return qt[u - 4, tile, :, lanes]

    def mates(u):
        dim, n, _ = along(u)
        flip = n + 1 - 2 * (n % 2)
        mirror = 3 - n
        return ((flip, mirror), (mirror, flip))

    def ring(u, n):
        dim = along(u)[0]
        return device(n if dim == 0 else cx, n if dim == 1 else cy, cz, core)

    def last_mate(u):
        if u < 4:
            return device(cx, cy, (1 - zh) * 2 + zl, core)
        return device(cx, cy, zh * 2 + (1 - zl), core)

    @jax.named_scope("step1")
    def step1(u):
        sem = group()
        for c in range(2):
            first, _ = mates(u)[c]
            flip = first + 1 - 2 * (first % 2)
            beyond = (3 - first) if c == 0 else flip
            for j in range(4):
                n = first if j < 2 else beyond
                s1[slot[u], c, j] = part_of(u, j % 2, n, c).astype(BF)
            flight[u, 1] = send(s1.at[slot[u], c], r1.at[slot[u], c], ring(u, first), 3, sem, r1.at[slot[u]])

    @jax.named_scope("step2")
    def step2(u):
        sem = group()
        arrived(flight[u, 1])
        for c in range(2):
            _, second = mates(u)[c]
            for j in range(2):
                s2[slot[u], c, j] = (part_of(u, j, second, c) + r1[slot[u], c, 2 + j].astype(F32)).astype(BF)
            flight[u, 2] = send(s2.at[slot[u], c], r2.at[slot[u], c], ring(u, second), 4, sem, r2.at[slot[u]])

    @jax.named_scope("step3")
    def step3(u):
        sem = group()
        _, n, z = along(u)
        arrived(flight[u, 2])
        for c in range(2):
            far = part_of(u, 1 - z, n, c) + r1[slot[u], c, 1 - z].astype(F32) + r2[slot[u], c, 1 - z].astype(F32)
            s3[slot[u], c] = far.astype(BF)
            flight[u, 3] = send(s3.at[slot[u], c], r3.at[slot[u], c], last_mate(u), 5, sem, r3.at[slot[u]])

    @jax.named_scope("finish")
    def finish(u):
        _, n, z = along(u)
        s = 3 if u < 4 else 2
        at = 48 * (u % 4)
        arrived(flight[u, 3])
        for c in range(2):
            total = part_of(u, z, n, c) + r1[slot[u], c, z].astype(F32) + r2[slot[u], c, z].astype(F32)
            total = (total + r3[slot[u], c].astype(F32)) * 0.0625
            stage[s, at:at + 48, 128 * c:128 * c + 128] = total.astype(BF)

    def whole_part(u, z, n):
        return kt[u, core, z * 4 + n] if u < 4 else qt[u - 4, z * 4 + n]

    @jax.named_scope("scatter")
    def scatter(u):
        dim, n, _ = along(u)
        e = place[u]
        sem = group()
        for k in range(4):
            for z in range(2):
                e1s[e, k, z] = whole_part(u, z, k).astype(BF)
        for d in (1, 2, 3):
            flight[u, 1] = send(
                e1s.at[e, (n + d) % 4], e1r.at[e, d - 1], shift(dim, d), 13, sem, e1r.at[e]
            )

    @jax.named_scope("pair")
    def pair(u):
        _, n, z = along(u)
        e = place[u]
        arrived(flight[u, 1])
        far = whole_part(u, 1 - z, n)
        for k in range(3):
            far = far + e1r[e, k, 1 - z].astype(F32)
        e2s[e] = far.astype(BF)
        flight[u, 2] = send(e2s.at[e], e2r.at[e], last_mate(u), 14, group(), e2r.at[e])

    @jax.named_scope("pair_finish")
    def pair_finish(u):
        _, n, z = along(u)
        e = place[u]
        total = whole_part(u, z, n)
        for k in range(3):
            total = total + e1r[e, k, z].astype(F32)
        arrived(flight[u, 2])
        at = 48 * (u % 4)
        stage[3 if u < 4 else 2, at:at + 48, :] = ((total + e2r[e].astype(F32)) * 0.0625).astype(BF)

    @jax.named_scope("direct")
    def direct():
        n = group()
        for k in range(8):
            d0s[k] = qt[3, k].astype(BF)
        for dz in range(2):
            for dx in range(4):
                if dz + dx:
                    z, x = (zl + dz) % 2, (cx + dx) % 4
                    flight[7, 1] = send(
                        d0s.at[z * 4 + x], d0r.at[dz * 4 + dx - 1], device(x, cy, zh * 2 + z, core), 12, n, d0r
                    )

    @jax.named_scope("direct_finish")
    def direct_finish():
        arrived(flight[7, 1])
        total = qt[3, zl * 4 + cx]
        for k in range(7):
            total = total + d0r[k].astype(F32)
        stage[2, 144:192, :] = (total * 0.0625).astype(BF)

    @jax.named_scope("core_step")
    def core_step(u):
        arrived(flight[u, 0])
        kt[u, core] = kt[u, core] + c0r[u]
        if u == 3:
            scatter(u)
        else:
            step1(u)

    @jax.named_scope("image_windows")
    def image_windows(s):
        padt[s] = dot_nt(eye[...], padded(s)).astype(BF)
        v = col(192)
        if s == 0:
            i = div(v, 24)
            f = i * 26 + (v - i * 24)
        else:
            j = div(v, 12)
            f = (v - j * 12) * 18 + j
        for rs in range(3):
            for cs in range(3):
                sel = select(f + tap_offset(s, rs, cs), QP)
                win_t[s, rs * 3 + cs] = dot_nt(padt[s], sel).astype(BF)

    @jax.named_scope("weight_part")
    def weight_part(s, first):
        for t in range(9):
            term = dot(win_t[s, t], stage[s + 2, 0:192, :])
            j, k = t // 3, t % 3
            for h in range(2):
                half = term[:, 128 * h:128 * h + 128]
                rows = slice(256 * k, 256 * k + 256)
                wacc[h, j, rows] = half if first else wacc[h, j, rows] + half
            if not first and k == 2:
                f0.append(send(wacc.at[1 - core, j], a0r.at[j], other_core, 6, group(), a0r.at[j]))

    @jax.named_scope("input_grad")
    def input_grad(s, slot):
        pad = padded(s)
        v = col(192)
        if s == 2:
            i = div(v, 24)
            f = i * 26 + (v - i * 24)
        else:
            f = lax.shift_right_logical(v, 4) * 18 + (v & 15)
        acc = jnp.zeros((192, 256), F32)
        for rs in range(3):
            for cs in range(3):
                sel = select(f + tap_offset(s, 2 - rs, 2 - cs), QP)
                win = dot(sel, pad).astype(BF)
                at = 256 * (rs * 3 + cs)
                acc = acc + dot_nt(win, cw[at:at + 256, :])
        ogs[slot] = acc.astype(BF)

    f0 = []
    tables()
    pool_keys()
    ld_q.wait()
    ld_gc.wait()
    coarse_levels()
    ld_g[0].wait()
    key_rows(0)
    key_tiles(0)
    for c in ld_img:
        c.wait()
    pl.semaphore_wait(barrier, len(partners))
    core_send(0)
    hc = [halo_cols(0), halo_cols(1)]

    def keys(i):
        if i < 3:
            ld_g[i].wait()
        key_rows(i)
        key_tiles(i)
        core_send(i)

    def queries(i):
        query_chunk(i)
        step1(4 + i)

    keys(1)
    core_step(0)
    keys(2)
    core_step(1)
    ld_g[3].wait()
    keys(3)
    core_step(2)
    queries(0)
    core_step(3)
    step2(0)
    hr = []
    for s in range(2):
        arrived(hc[s])
        hr.append(halo_rows(s))
    queries(1)
    step2(1)
    query_chunk(2)
    step2(2)
    step2(4)
    scatter(6)
    query_chunk(3)
    step2(5)
    direct()
    pair(3)
    step3(0)
    step3(1)
    arrived(hr[1])
    image_windows(1)
    step3(2)
    step3(4)
    arrived(hr[0])
    image_windows(0)
    pair(6)
    step3(5)
    for u in range(3):
        finish(u)
    pair_finish(3)
    hk = halo_cols(3)
    weight_part(1, True)
    for u in range(4, 6):
        finish(u)
    pair_finish(6)
    direct_finish()
    hq = halo_cols(2)
    weight_part(0, False)

    coords = (cx, cy, cz)
    f1 = []
    for j in range(3):
        arrived(f0[j])
        n = coords[j]
        wacc[core, j] = wacc[core, j] + a0r[j]
        for k in range(4):
            a1s[j, k] = wacc[core, j, 192 * k:192 * k + 192].astype(BF)
        sem = group()
        for d in (1, 2, 3):
            last = send(a1s.at[j, (n + d) % 4], a1r.at[j, d - 1], shift(j, d), 7, sem, a1r.at[j])
        f1.append(last)
    arrived(hk)
    hk = halo_rows(3)
    ld_cw.wait()
    f2 = []
    for j in range(3):
        arrived(f1[j])
        x = wacc[core, j, pl.ds(pl.multiple_of(192 * coords[j], 192), 192), :]
        for d in range(3):
            x = x + a1r[j, d].astype(F32)
        a2[j, 0] = x.astype(BF)
        sem = group()
        for d in (1, 2, 3):
            last = send(a2.at[j, 0], a2.at[j, d], shift((j + 1) % 3, d), 8, sem, a2.at[j, pl.ds(1, 3)])
        f2.append(last)
    arrived(hq)
    hq = halo_rows(2)
    arrived(hk)
    input_grad(3, 1)

    def ring_sum(ref, n):
        y = ref[n].astype(F32)
        for k in (1, 2, 3):
            y = y + ref[(n + 4 - k) % 4].astype(F32)
        return y.astype(BF)

    f3 = []
    for j in range(3):
        arrived(f2[j])
        a3[j, 0] = ring_sum(a2.at[j], coords[(j + 1) % 3])
        sem = group()
        for d in (1, 2, 3):
            last = send(a3.at[j, 0], a3.at[j, d], shift((j + 2) % 3, d), 9, sem, a3.at[j, pl.ds(1, 3)])
        f3.append(last)
    arrived(hq)
    input_grad(2, 0)
    copies = [load(ogs, og_out)]
    f5 = []
    own = []
    for j in range(3):
        arrived(f3[j])
        a4[j] = ring_sum(a3.at[j], coords[(j + 2) % 3])
        mine = w_out.at[core, j, coords[j]]
        sem = group()
        for d in (1, 2, 3):
            last = send(a4.at[j], mine, shift(j, d), 10, sem, a1r.at[j])
        f5.append(last)
        own.append(load(a4.at[j], mine))
    f6 = []
    for j in range(3):
        arrived(f5[j])
        own[j].wait()
        mine = w_out.at[core, j]
        f6.append(send(mine, mine, other_core, 11, group(), mine))
    for j in range(3):
        arrived(f6[j])
    sent = (colp, rowp, c0r, s1, s2, s3, a0r, a1r, a1r, a1r, a1r, a1s, d0r, e1r, e2r)
    for k, ref in enumerate(sent):
        pltpu.make_async_copy(ref, ref, send_sem.at[k]).wait()
    copies[0].wait()


def widen(og, w, qg_out, kg_out, w_out, wide, sem):
    copies = [
        pltpu.make_async_copy(og.at[0], qg_out, sem.at[0]),
        pltpu.make_async_copy(og.at[1], kg_out, sem.at[1]),
    ]
    for k in range(6):
        rows = pl.ds(384 * k, 384)
        for h in range(2):
            wide[384 * k:384 * k + 384, 128 * h:128 * h + 128] = w[h, 384 * k:384 * k + 384, :].astype(F32)
        copies.append(pltpu.make_async_copy(wide.at[rows], w_out.at[rows], sem.at[2 + k]))
        if k == 0:
            copies[0].start()
            copies[1].start()
        copies[-1].start()
    for c in copies:
        c.wait()


def vmem(*shape, dtype=BF):
    return pltpu.VMEM(shape, dtype)


def body(query_features, key_features, pyramid_grad, query_image, key_image, conv_weight):
    cells = jnp.transpose(pyramid_grad.reshape(QN, CELLS))
    anywhere = pl.BlockSpec(memory_space=pl.ANY)
    og, w = pl.pallas_call(
        kernel,
        out_shape=(
            jax.ShapeDtypeStruct((2, 192, 256), BF),
            jax.ShapeDtypeStruct((2, 3, 4, 192, 128), BF),
        ),
        in_specs=[pl.BlockSpec(memory_space=pltpu.HBM)] * 6,
        out_specs=[pl.BlockSpec(memory_space=pl.ANY)] * 2,
        scratch_shapes=[
            vmem(4096, QN), vmem(QN, 256), vmem(3072, 256), vmem(2304, 256),
            vmem(4096, 256), vmem(256, 4096), vmem(768, 256), vmem(2, 768, 256, dtype=F32),
            vmem(4, 2, 8, 48, 256, dtype=F32), vmem(4, 8, 48, 256, dtype=F32),
            vmem(4, 8, 48, 256, dtype=F32),
            vmem(5, 2, 4, 48, 128), vmem(5, 2, 4, 48, 128),
            vmem(5, 2, 2, 48, 128), vmem(5, 2, 2, 48, 128),
            vmem(5, 2, 48, 128), vmem(5, 2, 48, 128),
            vmem(8, 48, 256), vmem(7, 48, 256),
            vmem(2, 4, 2, 48, 256), vmem(2, 3, 2, 48, 256), vmem(2, 48, 256), vmem(2, 48, 256),
            vmem(256, 256), vmem(256, 256), vmem(128, 512), vmem(64, 1024), vmem(48, 3072),
            vmem(192, 48), vmem(768, 192), vmem(768, 192),
            vmem(4, ST, 256), vmem(4, 32, 256), vmem(4, 64, 256),
            vmem(2, 256, QP), vmem(2, 9, 256, 192), vmem(2, 3, 768, 128, dtype=F32),
            vmem(3, 768, 128, dtype=F32),
            vmem(3, 4, 192, 128), vmem(3, 3, 192, 128),
            vmem(3, 4, 192, 128), vmem(3, 4, 192, 128), vmem(3, 192, 128), vmem(2, 192, 256),
            pltpu.SemaphoreType.DMA((16,)),
            pltpu.SemaphoreType.DMA((15,)),
            pltpu.SemaphoreType.DMA((50,)),
        ],
        compiler_params=pltpu.CompilerParams(
            collective_id=0, has_side_effects=True, vmem_limit_bytes=VMEM_BYTES
        ),
    )(
        *[
            pltpu.with_memory_space_constraint(x, pltpu.HBM)
            for x in (
                cells,
                query_features.reshape(QN, 256),
                key_features.reshape(3072, 256),
                query_image.reshape(192, 256),
                key_image.reshape(192, 256),
                conv_weight.reshape(2304, 256),
            )
        ]
    )
    qg, kg, w = pl.pallas_call(
        widen,
        out_shape=(
            jax.ShapeDtypeStruct((192, 256), BF),
            jax.ShapeDtypeStruct((192, 256), BF),
            jax.ShapeDtypeStruct((2304, 256), F32),
        ),
        in_specs=[pl.BlockSpec(memory_space=pltpu.VMEM)] * 2,
        out_specs=[pl.BlockSpec(memory_space=pltpu.HBM)] * 3,
        scratch_shapes=[vmem(2304, 256, dtype=F32), pltpu.SemaphoreType.DMA((8,))],
        compiler_params=pltpu.CompilerParams(vmem_limit_bytes=16 * 1024 * 1024),
    )(og, w.reshape(2, 2304, 128))
    return qg.reshape(8, 24, 256), kg.reshape(12, 16, 256), w.reshape(3, 3, 256, 256)


def solution(mesh):
    placed = (
        P("pb", None, None),
        P(None, "ka", None),
        P("pb", "ka", None),
        P("pb", "ka", None),
        P("pb", "ka", None),
        P(),
    )
    return jax.shard_map(
        body,
        mesh=mesh,
        in_specs=placed,
        out_specs=(P("pb", "ka", None), P("pb", "ka", None), P()),
        check_vma=False,
    )
```

```python
import jax
import jax.numpy as jnp
from jax import lax
from jax.experimental import pallas as pl
from jax.experimental.pallas import tpu as pltpu
from jax.sharding import PartitionSpec as P

BF = jnp.bfloat16
F32 = jnp.float32
MESH = pl.DeviceIdType.MESH
CELLS = 4080
QN = 1536
VMEM_BYTES = 50 * 1024 * 1024
QP = 384
ST = 384
NT = (((1,), (1,)), ((), ()))


def dot(a, b):
    return jnp.dot(a, b, preferred_element_type=F32)


def dot_nt(a, b):
    return lax.dot_general(a, b, NT, preferred_element_type=F32)


def div(v, d):
    return lax.shift_right_logical(v * (-(-(1 << 20) // d)), 20)


def col(n):
    return lax.broadcasted_iota(jnp.int32, (n, 1), 0)


def row(n):
    return lax.broadcasted_iota(jnp.int32, (1, n), 1)


def select(src, n, value=1.0):
    wide = lax.broadcasted_iota(jnp.int32, (src.shape[0], n), 1)
    return jnp.where(wide == src, value, 0.0).astype(BF)


def pick(key, n, value):
    tall = lax.broadcasted_iota(jnp.int32, (n, key.shape[1]), 0)
    return jnp.where(tall == key, value, 0.0).astype(BF)


def kernel(
    g_hbm, q_hbm, k_hbm, qi_hbm, ki_hbm, cw_hbm,
    og_out, w_out,
    g, qv, kv, cw, pool, pool_t, mid, fine, kt, qt,
    c0r, s1, r1, s2, r2, s3, r3, d0s, d0r, e1s, e1r, e2s, e2r,
    eye, perm, mean1, mean2, mean3, up3, up2, up1,
    stage, colp, rowp, padt, win_t, wacc,
    a0s, a0r, a1s, a1r, a2, a3, a4, ogs,
    in_sem, send_sem, recv_sem,
):
    pb, ka = lax.axis_index("pb"), lax.axis_index("ka")
    core = pb % 2
    cy = (pb // 2) % 4
    zh = pb // 8
    cx = ka % 4
    zl = ka // 4
    cz = zh * 2 + zl

    def device(x, y, z, c):
        return {"pb": ((z // 2) * 4 + y) * 2 + c, "ka": (z % 2) * 4 + x}

    def shift(dim, d):
        return device(
            (cx + d) % 4 if dim == 0 else cx,
            (cy + d) % 4 if dim == 1 else cy,
            (cz + d) % 4 if dim == 2 else cz,
            core,
        )

    other_core = device(cx, cy, cz, 1 - core)
    pb_up = {"pb": (pb + 15) % 16, "ka": ka}
    pb_down = {"pb": (pb + 1) % 16, "ka": ka}
    ka_up = {"pb": pb, "ka": (ka + 7) % 8}
    ka_down = {"pb": pb, "ka": (ka + 1) % 8}

    loads = []
    used = [0]

    def group():
        used[0] += 1
        return used[0] - 1

    def send(src, dst, dev, k, n, whole):
        pltpu.make_async_remote_copy(
            src_ref=src, dst_ref=dst, send_sem=send_sem.at[k], recv_sem=recv_sem.at[n],
            device_id=dev, device_id_type=MESH,
        ).start()
        return whole, n

    def arrived(item):
        whole, n = item
        pltpu.make_async_copy(whole, whole, recv_sem.at[n]).wait()

    def load(src, dst):
        copy = pltpu.make_async_copy(src, dst, in_sem.at[len(loads)])
        copy.start()
        loads.append(copy)
        return copy

    ld_k = [load(k_hbm.at[pl.ds(1024 * i, 1024)], kv.at[pl.ds(1024 * i, 1024)]) for i in range(3)]
    ld_q = load(q_hbm, qv)
    ld_gc = load(g_hbm.at[pl.ds(3072, 1008)], g.at[pl.ds(3072, 1008)])
    ld_img = [load(qi_hbm, stage.at[0, pl.ds(0, 192)]), load(ki_hbm, stage.at[1, pl.ds(0, 192)])]
    ld_g = [load(g_hbm.at[pl.ds(768 * i, 768)], g.at[pl.ds(768 * i, 768)]) for i in range(4)]
    ld_cw = load(cw_hbm, cw)

    barrier = pltpu.get_barrier_semaphore()
    partners = [other_core, pb_up, pb_down, ka_up, ka_down]
    partners += [shift(dim, d) for dim in range(3) for d in (1, 2, 3)]
    for partner in partners:
        pl.semaphore_signal(barrier, inc=1, device_id=partner, device_id_type=MESH)

    for s in range(4):
        stage[s, 288:ST, :] = jnp.zeros((ST - 288, 256), BF)
    g[CELLS:4096, :] = jnp.zeros((4096 - CELLS, QN), BF)
    pool[CELLS:4096, :] = jnp.zeros((4096 - CELLS, 256), BF)

    rows_of = (8, 12, 8, 12)
    cols_of = (24, 16, 24, 16)

    def tile_index(s, i, j):
        return j * 12 + i if s == 3 else i * cols_of[s] + j

    @jax.named_scope("halo_cols")
    def halo_cols(s):
        n_r, n_c = rows_of[s], cols_of[s]
        v = col(32)
        i = v & 15
        src = jnp.where(v < 16, tile_index(s, i, 0), tile_index(s, i, n_c - 1))
        src = jnp.where(i < n_r, src, -1)
        colp[s] = dot(select(src, 192), stage[s, 0:192, :]).astype(BF)
        n = group()
        whole = stage.at[s, pl.ds(192, 32)]
        send(colp.at[s, pl.ds(0, 16)], stage.at[s, pl.ds(208, 16)], ka_up, 0, n, whole)
        return send(colp.at[s, pl.ds(16, 16)], stage.at[s, pl.ds(192, 16)], ka_down, 0, n, whole)

    @jax.named_scope("halo_rows")
    def halo_rows(s):
        n_r, n_c = rows_of[s], cols_of[s]
        v = col(64)
        j = (v & 31) - 1
        i = jnp.where(v < 32, 0, n_r - 1)
        src = tile_index(s, i, j)
        src = jnp.where(j < 0, jnp.where(ka == 0, -1, 192 + i), src)
        src = jnp.where(j == n_c, jnp.where(ka == 7, -1, 208 + i), src)
        src = jnp.where(j > n_c, -1, src)
        rowp[s] = dot(select(src, 224), stage[s, 0:224, :]).astype(BF)
        n = group()
        whole = stage.at[s, pl.ds(224, 64)]
        send(rowp.at[s, pl.ds(0, 32)], stage.at[s, pl.ds(256, 32)], pb_up, 1, n, whole)
        return send(rowp.at[s, pl.ds(32, 32)], stage.at[s, pl.ds(224, 32)], pb_down, 1, n, whole)

    def padded(s):
        n_r, n_c = rows_of[s], cols_of[s]
        v = col(QP)
        ip = div(v, n_c + 2)
        jp = v - ip * (n_c + 2)
        i, j = ip - 1, jp - 1
        src = tile_index(s, i, j)
        src = jnp.where(j < 0, jnp.where(ka == 0, -1, 192 + i), src)
        src = jnp.where(j == n_c, jnp.where(ka == 7, -1, 208 + i), src)
        src = jnp.where(i < 0, jnp.where(pb == 0, -1, 224 + jp), src)
        src = jnp.where(i == n_r, jnp.where(pb == 15, -1, 256 + jp), src)
        src = jnp.where(i > n_r, -1, src)
        return dot(select(src, ST), stage[s]).astype(BF)

    def tap_offset(s, rs, cs):
        pitch = cols_of[s] + 2
        return cs * pitch + rs if s % 2 else rs * pitch + cs

    flight = {}
    slot = {0: 0, 1: 1, 2: 2, 4: 3, 5: 4}
    place = {3: 0, 6: 1}

    @jax.named_scope("tables")
    def tables():
        o = col(256)
        eye[...] = select(o, 256)
        perm[...] = select((o & 15) * 16 + lax.shift_right_logical(o, 4), 256)
        k = row(512)
        mean1[...] = pick(lax.shift_right_logical(k & 15, 1) * 16 + lax.shift_right_logical(k, 5), 128, 0.25)
        k = row(1024)
        mean2[...] = pick(lax.shift_right_logical(k & 15, 2) * 16 + lax.shift_right_logical(k, 6), 64, 0.0625)
        k = row(3072)
        key = (lax.shift_right_logical(k, 3) & 1) * 24 + lax.shift_right_logical(k, 7)
        mean3[...] = pick(key, 48, 0.015625)
        v = col(192)
        r = div(v, 48)
        up3[...] = select(lax.shift_right_logical(r, 1) * 24 + lax.shift_right_logical(v - r * 48, 1), 48)
        v = col(768)
        r = div(v, 96)
        up2[...] = select(lax.shift_right_logical(r, 1) * 48 + lax.shift_right_logical(v - r * 96, 1), 192)
        r = div(v, 192)
        up1[...] = select(lax.shift_right_logical(r, 1) * 96 + lax.shift_right_logical(v - r * 192, 1), 192)

    @jax.named_scope("pool_keys")
    def pool_keys():
        for b in range(12):
            if b % 4 == 0:
                ld_k[b // 4].wait()
            block = dot(perm[...], kv[256 * b:256 * b + 256, :]).astype(BF)
            for r in range(16):
                pool[192 * r + 16 * b:192 * r + 16 * b + 16, :] = block[16 * r:16 * r + 16, :]
        for b in range(6):
            block = dot(mean1[...], kv[512 * b:512 * b + 512, :]).astype(BF)
            for r in range(8):
                at = 3072 + 96 * r + 16 * b
                pool[at:at + 16, :] = block[16 * r:16 * r + 16, :]
        for b in range(3):
            block = dot(mean2[...], kv[1024 * b:1024 * b + 1024, :]).astype(BF)
            for r in range(4):
                at = 3840 + 48 * r + 16 * b
                pool[at:at + 16, :] = block[16 * r:16 * r + 16, :]
        pool[4032:4080, :] = dot(mean3[...], kv[...]).astype(BF)
        for b in range(16):
            pool_t[:, 256 * b:256 * b + 256] = dot_nt(eye[...], pool[256 * b:256 * b + 256, :]).astype(BF)

    @jax.named_scope("coarse_levels")
    def coarse_levels():
        l3 = (dot(g[4032:4080, :], qv[...]) * (1.0 / 64.0)).astype(BF)
        l2 = (dot(g[3840:4032, :], qv[...]) * (1.0 / 16.0) + dot(up3[...], l3)).astype(BF)
        for k in range(3):
            at = 256 * k
            part = dot(g[3072 + at:3328 + at, :], qv[...]) * 0.25 + dot(up2[at:at + 256, :], l2)
            mid[at:at + 256, :] = part.astype(BF)

    @jax.named_scope("key_rows")
    def key_rows(i):
        right = jnp.concatenate([qv[...], mid[192 * i:192 * i + 192, :]], axis=0)
        for k in range(3):
            at = 768 * i + 256 * k
            left = jnp.concatenate([g[at:at + 256, :], up1[256 * k:256 * k + 256, :]], axis=1)
            fine[i % 2, 256 * k:256 * k + 256, :] = dot(left, right)

    def key_tiles(i):
        for t in range(8):
            for p in range(2):
                for r in range(4):
                    at = 192 * r + 24 * t + 12 * p
                    kt[i, p, t, 12 * r:12 * r + 12, :] = fine[i % 2, at:at + 12, :]

    def core_send(i):
        flight[i, 0] = send(kt.at[i, 1 - core], c0r.at[i], other_core, 2, group(), c0r.at[i])

    @jax.named_scope("query_chunk")
    def query_chunk(i):
        part = dot(pool_t[...], g[:, 384 * i:384 * i + 384])
        part = jnp.transpose(part)
        for hh in range(2):
            for k in range(8):
                at = 192 * hh + 24 * k
                qt[i, k, 24 * hh:24 * hh + 24, :] = part[at:at + 24, :]

    def along(u):
        return (1, cy, zh) if u < 4 else (0, cx, zl)

    def part_of(u, g_, n, c):
        lanes = slice(128 * c, 128 * c + 128)
        tile = g_ * 4 + n
        if u < 4:
            return kt[u, core, tile, :, lanes]
        return qt[u - 4, tile, :, lanes]

    def mates(u):
        dim, n, _ = along(u)
        flip = n + 1 - 2 * (n % 2)
        mirror = 3 - n
        return ((flip, mirror), (mirror, flip))

    def ring(u, n):
        dim = along(u)[0]
        return device(n if dim == 0 else cx, n if dim == 1 else cy, cz, core)

    def last_mate(u):
        if u < 4:
            return device(cx, cy, (1 - zh) * 2 + zl, core)
        return device(cx, cy, zh * 2 + (1 - zl), core)

    @jax.named_scope("step1")
    def step1(u):
        sem = group()
        for c in range(2):
            first, _ = mates(u)[c]
            flip = first + 1 - 2 * (first % 2)
            beyond = (3 - first) if c == 0 else flip
            for j in range(4):
                n = first if j < 2 else beyond
                s1[slot[u], c, j] = part_of(u, j % 2, n, c).astype(BF)
            flight[u, 1] = send(s1.at[slot[u], c], r1.at[slot[u], c], ring(u, first), 3, sem, r1.at[slot[u]])

    @jax.named_scope("step2")
    def step2(u):
        sem = group()
        arrived(flight[u, 1])
        for c in range(2):
            _, second = mates(u)[c]
            for j in range(2):
                s2[slot[u], c, j] = (part_of(u, j, second, c) + r1[slot[u], c, 2 + j].astype(F32)).astype(BF)
            flight[u, 2] = send(s2.at[slot[u], c], r2.at[slot[u], c], ring(u, second), 4, sem, r2.at[slot[u]])

    @jax.named_scope("step3")
    def step3(u):
        sem = group()
        _, n, z = along(u)
        arrived(flight[u, 2])
        for c in range(2):
            far = part_of(u, 1 - z, n, c) + r1[slot[u], c, 1 - z].astype(F32) + r2[slot[u], c, 1 - z].astype(F32)
            s3[slot[u], c] = far.astype(BF)
            flight[u, 3] = send(s3.at[slot[u], c], r3.at[slot[u], c], last_mate(u), 5, sem, r3.at[slot[u]])

    @jax.named_scope("finish")
    def finish(u):
        _, n, z = along(u)
        s = 3 if u < 4 else 2
        at = 48 * (u % 4)
        arrived(flight[u, 3])
        for c in range(2):
            total = part_of(u, z, n, c) + r1[slot[u], c, z].astype(F32) + r2[slot[u], c, z].astype(F32)
            total = (total + r3[slot[u], c].astype(F32)) * 0.0625
            stage[s, at:at + 48, 128 * c:128 * c + 128] = total.astype(BF)

    def whole_part(u, z, n):
        return kt[u, core, z * 4 + n] if u < 4 else qt[u - 4, z * 4 + n]

    @jax.named_scope("scatter")
    def scatter(u):
        dim, n, _ = along(u)
        e = place[u]
        sem = group()
        for k in range(4):
            for z in range(2):
                e1s[e, k, z] = whole_part(u, z, k).astype(BF)
        for d in (1, 2, 3):
            flight[u, 1] = send(
                e1s.at[e, (n + d) % 4], e1r.at[e, d - 1], shift(dim, d), 13, sem, e1r.at[e]
            )

    @jax.named_scope("pair")
    def pair(u):
        _, n, z = along(u)
        e = place[u]
        arrived(flight[u, 1])
        far = whole_part(u, 1 - z, n)
        for k in range(3):
            far = far + e1r[e, k, 1 - z].astype(F32)
        e2s[e] = far.astype(BF)
        flight[u, 2] = send(e2s.at[e], e2r.at[e], last_mate(u), 14, group(), e2r.at[e])

    @jax.named_scope("pair_finish")
    def pair_finish(u):
        _, n, z = along(u)
        e = place[u]
        total = whole_part(u, z, n)
        for k in range(3):
            total = total + e1r[e, k, z].astype(F32)
        arrived(flight[u, 2])
        at = 48 * (u % 4)
        stage[3 if u < 4 else 2, at:at + 48, :] = ((total + e2r[e].astype(F32)) * 0.0625).astype(BF)

    @jax.named_scope("direct")
    def direct():
        n = group()
        for k in range(8):
            d0s[k] = qt[3, k].astype(BF)
        for dz in range(2):
            for dx in range(4):
                if dz + dx:
                    z, x = (zl + dz) % 2, (cx + dx) % 4
                    flight[7, 1] = send(
                        d0s.at[z * 4 + x], d0r.at[dz * 4 + dx - 1], device(x, cy, zh * 2 + z, core), 12, n, d0r
                    )

    @jax.named_scope("direct_finish")
    def direct_finish():
        arrived(flight[7, 1])
        total = qt[3, zl * 4 + cx]
        for k in range(7):
            total = total + d0r[k].astype(F32)
        stage[2, 144:192, :] = (total * 0.0625).astype(BF)

    @jax.named_scope("core_step")
    def core_step(u):
        arrived(flight[u, 0])
        kt[u, core] = kt[u, core] + c0r[u]
        if u == 3:
            scatter(u)
        else:
            step1(u)

    @jax.named_scope("image_windows")
    def image_windows(s):
        padt[s] = dot_nt(eye[...], padded(s)).astype(BF)
        v = col(192)
        if s == 0:
            i = div(v, 24)
            f = i * 26 + (v - i * 24)
        else:
            j = div(v, 12)
            f = (v - j * 12) * 18 + j
        for rs in range(3):
            for cs in range(3):
                sel = select(f + tap_offset(s, rs, cs), QP)
                win_t[s, rs * 3 + cs] = dot_nt(padt[s], sel).astype(BF)

    @jax.named_scope("weight_part")
    def weight_part(s, first):
        for t in range(9):
            term = dot(win_t[s, t], stage[s + 2, 0:192, :])
            j, k = t // 3, t % 3
            for h in range(2):
                half = term[:, 128 * h:128 * h + 128]
                rows = slice(256 * k, 256 * k + 256)
                wacc[h, j, rows] = half if first else wacc[h, j, rows] + half
            if not first and k == 2:
                a0s[j] = wacc[1 - core, j].astype(BF)
                f0.append(send(a0s.at[j], a0r.at[j], other_core, 6, group(), a0r.at[j]))

    @jax.named_scope("input_grad")
    def input_grad(s, slot):
        pad = padded(s)
        v = col(192)
        if s == 2:
            i = div(v, 24)
            f = i * 26 + (v - i * 24)
        else:
            f = lax.shift_right_logical(v, 4) * 18 + (v & 15)
        acc = jnp.zeros((192, 256), F32)
        for rs in range(3):
            for cs in range(3):
                sel = select(f + tap_offset(s, 2 - rs, 2 - cs), QP)
                win = dot(sel, pad).astype(BF)
                at = 256 * (rs * 3 + cs)
                acc = acc + dot_nt(win, cw[at:at + 256, :])
        ogs[slot] = acc.astype(BF)

    f0 = []
    tables()
    pool_keys()
    ld_q.wait()
    ld_gc.wait()
    coarse_levels()
    ld_g[0].wait()
    key_rows(0)
    key_tiles(0)
    for c in ld_img:
        c.wait()
    pl.semaphore_wait(barrier, len(partners))
    core_send(0)
    hc = [halo_cols(0), halo_cols(1)]

    def keys(i):
        if i < 3:
            ld_g[i].wait()
        key_rows(i)
        key_tiles(i)
        core_send(i)

    def queries(i):
        query_chunk(i)
        step1(4 + i)

    keys(1)
    core_step(0)
    keys(2)
    core_step(1)
    ld_g[3].wait()
    keys(3)
    core_step(2)
    queries(0)
    core_step(3)
    step2(0)
    hr = []
    for s in range(2):
        arrived(hc[s])
        hr.append(halo_rows(s))
    queries(1)
    step2(1)
    query_chunk(2)
    step2(2)
    step2(4)
    scatter(6)
    query_chunk(3)
    step2(5)
    direct()
    pair(3)
    step3(0)
    step3(1)
    arrived(hr[1])
    image_windows(1)
    step3(2)
    step3(4)
    arrived(hr[0])
    image_windows(0)
    pair(6)
    step3(5)
    for u in range(3):
        finish(u)
    pair_finish(3)
    hk = halo_cols(3)
    weight_part(1, True)
    for u in range(4, 6):
        finish(u)
    pair_finish(6)
    direct_finish()
    hq = halo_cols(2)
    weight_part(0, False)

    coords = (cx, cy, cz)
    f1 = []
    for j in range(3):
        arrived(f0[j])
        n = coords[j]
        wacc[core, j] = wacc[core, j] + a0r[j].astype(F32)
        for k in range(4):
            a1s[j, k] = wacc[core, j, 192 * k:192 * k + 192].astype(BF)
        sem = group()
        for d in (1, 2, 3):
            last = send(a1s.at[j, (n + d) % 4], a1r.at[j, d - 1], shift(j, d), 7, sem, a1r.at[j])
        f1.append(last)
    arrived(hk)
    hk = halo_rows(3)
    ld_cw.wait()
    f2 = []
    for j in range(3):
        arrived(f1[j])
        x = wacc[core, j, pl.ds(pl.multiple_of(192 * coords[j], 192), 192), :]
        for d in range(3):
            x = x + a1r[j, d].astype(F32)
        a2[j, 0] = x.astype(BF)
        sem = group()
        for d in (1, 2, 3):
            last = send(a2.at[j, 0], a2.at[j, d], shift((j + 1) % 3, d), 8, sem, a2.at[j, pl.ds(1, 3)])
        f2.append(last)
    arrived(hq)
    hq = halo_rows(2)
    arrived(hk)
    input_grad(3, 1)

    def ring_sum(ref, n):
        y = ref[n].astype(F32)
        for k in (1, 2, 3):
            y = y + ref[(n + 4 - k) % 4].astype(F32)
        return y.astype(BF)

    f3 = []
    for j in range(3):
        arrived(f2[j])
        a3[j, 0] = ring_sum(a2.at[j], coords[(j + 1) % 3])
        sem = group()
        for d in (1, 2, 3):
            last = send(a3.at[j, 0], a3.at[j, d], shift((j + 2) % 3, d), 9, sem, a3.at[j, pl.ds(1, 3)])
        f3.append(last)
    arrived(hq)
    input_grad(2, 0)
    copies = [load(ogs, og_out)]
    f5 = []
    own = []
    for j in range(3):
        arrived(f3[j])
        a4[j] = ring_sum(a3.at[j], coords[(j + 2) % 3])
        mine = w_out.at[core, j, coords[j]]
        sem = group()
        for d in (1, 2, 3):
            last = send(a4.at[j], mine, shift(j, d), 10, sem, a1r.at[j])
        f5.append(last)
        own.append(load(a4.at[j], mine))
    f6 = []
    for j in range(3):
        arrived(f5[j])
        own[j].wait()
        mine = w_out.at[core, j]
        f6.append(send(mine, mine, other_core, 11, group(), mine))
    for j in range(3):
        arrived(f6[j])
    sent = (colp, rowp, c0r, s1, s2, s3, a0r, a1r, a1r, a1r, a1r, a1s, d0r, e1r, e2r)
    for k, ref in enumerate(sent):
        pltpu.make_async_copy(ref, ref, send_sem.at[k]).wait()
    copies[0].wait()


def widen(og, w, qg_out, kg_out, w_out, wide, sem):
    copies = [
        pltpu.make_async_copy(og.at[0], qg_out, sem.at[0]),
        pltpu.make_async_copy(og.at[1], kg_out, sem.at[1]),
    ]
    for k in range(6):
        rows = pl.ds(384 * k, 384)
        for h in range(2):
            wide[384 * k:384 * k + 384, 128 * h:128 * h + 128] = w[h, 384 * k:384 * k + 384, :].astype(F32)
        copies.append(pltpu.make_async_copy(wide.at[rows], w_out.at[rows], sem.at[2 + k]))
        if k == 0:
            copies[0].start()
            copies[1].start()
        copies[-1].start()
    for c in copies:
        c.wait()


def vmem(*shape, dtype=BF):
    return pltpu.VMEM(shape, dtype)


def body(query_features, key_features, pyramid_grad, query_image, key_image, conv_weight):
    cells = jnp.transpose(pyramid_grad.reshape(QN, CELLS))
    anywhere = pl.BlockSpec(memory_space=pl.ANY)
    og, w = pl.pallas_call(
        kernel,
        out_shape=(
            jax.ShapeDtypeStruct((2, 192, 256), BF),
            jax.ShapeDtypeStruct((2, 3, 4, 192, 128), BF),
        ),
        in_specs=[pl.BlockSpec(memory_space=pltpu.HBM)] * 6,
        out_specs=[pl.BlockSpec(memory_space=pl.ANY)] * 2,
        scratch_shapes=[
            vmem(4096, QN), vmem(QN, 256), vmem(3072, 256), vmem(2304, 256),
            vmem(4096, 256), vmem(256, 4096), vmem(768, 256), vmem(2, 768, 256, dtype=F32),
            vmem(4, 2, 8, 48, 256, dtype=F32), vmem(4, 8, 48, 256, dtype=F32),
            vmem(4, 8, 48, 256, dtype=F32),
            vmem(5, 2, 4, 48, 128), vmem(5, 2, 4, 48, 128),
            vmem(5, 2, 2, 48, 128), vmem(5, 2, 2, 48, 128),
            vmem(5, 2, 48, 128), vmem(5, 2, 48, 128),
            vmem(8, 48, 256), vmem(7, 48, 256),
            vmem(2, 4, 2, 48, 256), vmem(2, 3, 2, 48, 256), vmem(2, 48, 256), vmem(2, 48, 256),
            vmem(256, 256), vmem(256, 256), vmem(128, 512), vmem(64, 1024), vmem(48, 3072),
            vmem(192, 48), vmem(768, 192), vmem(768, 192),
            vmem(4, ST, 256), vmem(4, 32, 256), vmem(4, 64, 256),
            vmem(2, 256, QP), vmem(2, 9, 256, 192), vmem(2, 3, 768, 128, dtype=F32),
            vmem(3, 768, 128), vmem(3, 768, 128),
            vmem(3, 4, 192, 128), vmem(3, 3, 192, 128),
            vmem(3, 4, 192, 128), vmem(3, 4, 192, 128), vmem(3, 192, 128), vmem(2, 192, 256),
            pltpu.SemaphoreType.DMA((16,)),
            pltpu.SemaphoreType.DMA((15,)),
            pltpu.SemaphoreType.DMA((50,)),
        ],
        compiler_params=pltpu.CompilerParams(
            collective_id=0, has_side_effects=True, vmem_limit_bytes=VMEM_BYTES
        ),
    )(
        *[
            pltpu.with_memory_space_constraint(x, pltpu.HBM)
            for x in (
                cells,
                query_features.reshape(QN, 256),
                key_features.reshape(3072, 256),
                query_image.reshape(192, 256),
                key_image.reshape(192, 256),
                conv_weight.reshape(2304, 256),
            )
        ]
    )
    qg, kg, w = pl.pallas_call(
        widen,
        out_shape=(
            jax.ShapeDtypeStruct((192, 256), BF),
            jax.ShapeDtypeStruct((192, 256), BF),
            jax.ShapeDtypeStruct((2304, 256), F32),
        ),
        in_specs=[pl.BlockSpec(memory_space=pltpu.VMEM)] * 2,
        out_specs=[pl.BlockSpec(memory_space=pltpu.HBM)] * 3,
        scratch_shapes=[vmem(2304, 256, dtype=F32), pltpu.SemaphoreType.DMA((8,))],
        compiler_params=pltpu.CompilerParams(vmem_limit_bytes=16 * 1024 * 1024),
    )(og, w.reshape(2, 2304, 128))
    return qg.reshape(8, 24, 256), kg.reshape(12, 16, 256), w.reshape(3, 3, 256, 256)


def solution(mesh):
    placed = (
        P("pb", None, None),
        P(None, "ka", None),
        P("pb", "ka", None),
        P("pb", "ka", None),
        P("pb", "ka", None),
        P(),
    )
    return jax.shard_map(
        body,
        mesh=mesh,
        in_specs=placed,
        out_specs=(P("pb", "ka", None), P("pb", "ka", None), P()),
        check_vma=False,
    )
```
